128 devices in a mesh: row: 8 (over z, x_hi), col: 16 (over y, x_lo, core).
Axes of the slice: x: 4 (x_hi: 2, x_lo: 2; x = x_hi * 2 + x_lo), y: 4, z: 4, core: 2. Of those that a mesh axis runs over, the one named last changes fastest.
Arguments:
- trailing: float32 [16384, 16384], P('row', 'col'), may hold values from -6 to 6
- panel_factors: float32 [2048, 16384], P('col', 'row'), may hold values from -1.2 to 1.2
- vectors_t: float32 [32, 64, 512], P('col'), may hold values from -0.25 to 0.25
- inverse_lower_factors: float32 [32, 512, 512], P('col', 'row'), as said below
- slot_of_panel: int32 [32], replicated, may hold values from 0 to 31, each once
Outputs:
- updated: float32 [16384, 16384], P('row', 'col')
The draws below stay inside these ranges and needn't reach their ends.
Inputs may be any that keep to these rules, and one draw needn't show every extreme that they name: `slot_of_panel`: a permutation of the panels' slots. `inverse_lower_factors`: each slot's matrix is lower triangular with a positive diagonal.
All inputs are finite; a program needn't handle non-finite values.
Results may differ from the reference program's by a relative error of at most 0.000075.
Values sent between devices are 32-bit elements; how exact they have to be, the bound alone decides.
A program may use at most 256 MiB of HBM per device.

```python
import math
import jax
import jax.numpy as jnp
from jax import lax

ORDER = 16384
TILE = 512
RANK = 64
PANELS = 32


def draw_inverse_lower_factors(key, part):
    first, second, third = jax.random.split(jax.random.fold_in(key, 7), 3)
    rough = jax.random.normal(first, (PANELS, TILE, TILE), jnp.float32) * (0.6 / math.sqrt(TILE))
    diagonal_tile = jax.random.uniform(second, (PANELS, TILE), jnp.float32, 0.5, 2.0)
    factor = jnp.exp(jax.random.uniform(third, (PANELS, 1, 1), jnp.float32, -0.7, 0.7))
    lower = jnp.tril(rough, -1) + diagonal_tile[:, :, None] * jnp.eye(TILE, dtype=jnp.float32)[None, :, :]
    return lower * factor


def level_of(key, dims, pieces, low, high):
    def one(axis_at, shards_of):
        draws = jax.random.uniform(jax.random.fold_in(jax.random.fold_in(key, 6), axis_at), (shards_of,), jnp.float32, low / len(pieces), high / len(pieces))
        return jnp.repeat(jnp.exp(draws), dims[axis_at] // shards_of).reshape((-1,) + (1,) * (len(dims) - axis_at - 1))

    loudness = one(*pieces[0])
    for cut in pieces[1:]:
        loudness = loudness * one(*cut)
    return loudness


def scatter_about(key, shape, spread, most, cuts=(), kind=jnp.bfloat16):
    values = jax.random.normal(key, shape, jnp.float32) * spread
    if len(cuts) > 0:
        values = level_of(key, shape, cuts, -0.22, 0.18) * values
    return jnp.clip(values, min=-most, max=most).astype(kind)


def setup_inputs(seed: int = 0) -> dict:
    key_of = jax.random.split(jax.random.key(seed), 6)
    trailing = scatter_about(key_of[0], (ORDER, ORDER), 1.0, 6.0, ((0, 8), (1, 16)), jnp.float32)
    panel_factors = scatter_about(key_of[1], (PANELS * RANK, ORDER), 0.18, 1.2, ((0, 16), (1, 8)), jnp.float32)
    vectors_t = scatter_about(key_of[2], (PANELS, RANK, TILE), TILE ** -0.5, 0.25, ((0, 16),), jnp.float32)
    inverse_lower_factors = draw_inverse_lower_factors(jax.random.fold_in(key_of[5], 71), 0)
    slot_of_panel = jax.random.permutation(key_of[4], PANELS).astype(jnp.int32)
    return {"trailing": trailing, "panel_factors": panel_factors, "vectors_t": vectors_t, "inverse_lower_factors": inverse_lower_factors, "slot_of_panel": slot_of_panel}


def reference(trailing, panel_factors, vectors_t, inverse_lower_factors, slot_of_panel):
    highest_precision = lax.Precision.HIGHEST
    solved_panel = jnp.einsum("sat,srt->sar", vectors_t, inverse_lower_factors, precision=highest_precision)
    core_blocks = jnp.einsum("fdv,fpv->fdp", solved_panel, solved_panel, precision=highest_precision)
    panel_cores = core_blocks[slot_of_panel.astype(jnp.int32)]
    reshaped_block = panel_factors.reshape(PANELS, RANK, ORDER)
    scaled = jnp.einsum("pab,pbi->pai", panel_cores, reshaped_block, precision=highest_precision).reshape(PANELS * RANK, ORDER)
    update = lax.dot_general(scaled, panel_factors, (((0,), (0,)), ((), ())), precision=highest_precision)
    return trailing - update
```

```python
import jax
import jax.numpy as jnp
from jax import lax
from jax.experimental import pallas as pl
from jax.experimental.pallas import tpu as pltpu
from jax.sharding import PartitionSpec as P

MESH = pl.DeviceIdType.MESH
F32, BF16, I32 = jnp.float32, jnp.bfloat16, jnp.int32

ITEMS = (
    (16, 24720, 57394, 81938, 262224, 73745, 20785, 434192),
    (438273, 397332, 94864, 16435, 16497, 86482, 57362, 430224),
    (57346, 28674, 24947, 28672, 12386, 33219, 69747, 127106),
    (262196, 62034, 8210, 53554, 77875, 401412, 36865, 98387),
    (16464, 119363, 4240, 393717, 408659, 110641, 115538, 12417),
    (65571, 176710, 41138, 20946, 284692, 422672, 8881, 355666),
    (262181, 8656, 4259, 160198, 131094, 8402, 193190, 412997),
    (90768, 115138, 393349, 440337, 360720, 151750, 103154, 53714),
    (316037, 418244, 163974, 264196, 33025, 405620, 53987, 20723),
    (201350, 147910, 151718, 86544, 65795, 135270, 49937, 238022),
    (330803, 28883, 119026, 90627, 91122, 426544, 66307, 159974),
    (287156, 155846, 250086, 184838, 414693, 418341, 226022, 418416),
    (180646, 428049, 127328, 24690, 258310, 156198, 164614, 115297),
    (273776, 74610, 2071, 12387, 164838, 371955, 119074, 45667),
    (41106, 217958, 28978, 139366, 4195, 416996, 24674, 152166),
    (355346, 86147, 33059, 36944, 266384, 61475, 425168, 351538),
    (147590, 293301, 168230, 151622, 41090, 53330, 45138, 351344),
    (269523, 32898, 94850, 396307, 32899, 143430, 135238, 298081),
    (16387, 49683, 78322, 41874, 147590, 273584, 86195, 426896),
    (242614, 265488, 184806, 86915, 326802, 335009, 147622, 21378),
    (78000, 426036, 221910, 422789, 412787, 41395, 20530, 250758),
    (450721, 172070, 272629, 177030, 2775, 233894, 32803, 36930),
    (151718, 24914, 143446, 334036, 277268, 384275, 139302, 61571),
    (8466, 164166, 404016, 420369, 301829, 13009, 20851, 415921),
    (20739, 58163, 371236, 265584, 2903, 197318, 176486, 293028),
    (315652, 160022, 20483, 317716, 36929, 25346, 411889, 41651),
    (266501, 424657, 246678, 94499, 326835, 49681, 288996, 193190),
    (155910, 387781, 139382, 430421, 393941, 205318, 376051, 281810),
    (376050, 272949, 2487, 135494, 205510, 164182, 50162, 425157),
    (332020, 69635, 205206, 269520, 287152, 264213, 78819, 221718),
    (159974, 276533, 393812, 61922, 45473, 272469, 259046, 185142),
    (164054, 151670, 180806, 436273, 184742, 2359, 184758, 438576),
    (294352, 28672, 101396, 268324, 359666, 407761, 102497, 24866),
    (285971, 2903, 400389, 277681, 272436, 213686, 217590, 147750),
    (168246, 143446, 280628, 402357, 268325, 403953, 45347, 82643),
    (277810, 16560, 437201, 193446, 377328, 281061, 298064, 285364),
    (98992, 94371, 285841, 2487, 102881, 277520, 400452, 338597),
    (279204, 139430, 74002, 2135, 168422, 400389, 280756, 268404),
    (291493, 254358, 147718, 305716, 53315, 16626, 110801, 45058),
    (209574, 347376, 217782, 12432, 305844, 159974, 213190, 413744),
    (45394, 123682, 420177, 188550, 2135, 126004, 172374, 57379),
    (172358, 273521, 358724, 281936, 282960, 176406, 2071, 143398),
    (285778, 400402, 24930, 164086, 172358, 2807, 66193, 422832),
    (340340, 404338, 2135, 66290, 2647, 411793, 127619, 29602),
    (340325, 306257, 290128, 414437, 346324, 2103, 156294, 177062),
    (176486, 432369, 90930, 217830, 350405, 309364, 58177, 403472),
    (49264, 280805, 123683, 77858, 74289, 168086, 2103, 276485),
    (7, 205590, 234278, 118787, 2167, 7, 284948, 306450),
    (7, 2135, 32978, 2167, 7, 7, 289029, 428083),
    (7, 419952, 155846, 7, 7, 7, 2135, 318834),
    (7, 415841, 2167, 7, 7, 7, 188886, 433507),
    (7, 325973, 7, 7, 7, 7, 106499, 276564),
    (7, 74528, 7, 7, 7, 7, 151702, 66242),
    (7, 2199, 7, 7, 7, 7, 2167, 172310),
    (7, 7, 7, 7, 7, 7, 301205, 110802),
    (7, 7, 7, 7, 7, 7, 7, 200902),
    (7, 7, 7, 7, 7, 7, 7, 421045),
    (7, 7, 7, 7, 7, 7, 7, 294032),
    (7, 7, 7, 7, 7, 7, 7, 310401),
    (7, 7, 7, 7, 7, 7, 7, 139382),
    (7, 7, 7, 7, 7, 7, 7, 411985),
    (7, 7, 7, 7, 7, 7, 7, 164214),
    (446865, 2679, 115440, 143542, 37490, 209078, 396560, 343282),
    (344452, 434548, 94947, 107120, 41571, 28977, 433412, 7),
    (287109, 246118, 201446, 209510, 209510, 28962, 7, 7),
    (184710, 298129, 2199, 298035, 90289, 393508, 7, 7),
    (119282, 310576, 7, 2199, 151718, 172326, 7, 7),
    (188902, 2807, 7, 7, 297876, 32802, 7, 7),
    (106562, 7, 7, 7, 7, 7, 7, 7),
    (230198, 7, 7, 7, 7, 7, 7, 7),
    (384178, 222166, 7, 7, 2999, 2743, 52528, 7),
    (7, 7, 7, 7, 122946, 7, 330800, 7),
    (299076, 2231, 127858, 229974, 385328, 301236, 7, 60501),
    (7, 407763, 37731, 7, 98593, 94211, 7, 334324),
    (7, 358597, 197478, 7, 192806, 330388, 7, 301204),
    (7, 7, 2231, 7, 7, 7, 7, 305812),
    (7, 7, 426961, 7, 7, 7, 7, 49857),
    (7, 7, 238534, 7, 7, 7, 7, 7),
    (106960, 408757, 62387, 407729, 2295, 420721, 416305, 86194),
    (360900, 188662, 160678, 289396, 294098, 355173, 317988, 155814),
    (192966, 103344, 293365, 155862, 246742, 70609, 159990, 45057),
    (197142, 410532, 2263, 301428, 2199, 185286, 2263, 2263),
    (7, 242598, 7, 306321, 2231, 298192, 127890, 2295),
    (7, 7, 7, 310384, 409813, 180854, 111491, 7),
    (7, 7, 7, 254678, 155846, 314512, 234374, 7),
    (7, 7, 7, 2711, 321908, 326785, 74002, 7),
    (7, 7, 7, 127827, 295696, 82691, 229638, 7),
    (7, 7, 7, 213830, 217862, 250230, 321844, 7),
    (7, 7, 7, 123282, 49522, 321780, 7, 7),
    (7, 7, 7, 168326, 225638, 313573, 7, 7),
    (7, 7, 7, 172310, 314324, 65538, 7, 7),
    (7, 7, 7, 309556, 306117, 123474, 7, 7),
    (7, 7, 7, 2295, 311840, 201286, 7, 7),
    (7, 7, 7, 7, 106737, 7, 7, 7),
    (7, 7, 7, 7, 159974, 7, 7, 7),
    (7, 7, 7, 7, 188886, 7, 7, 7),
    (7, 7, 7, 7, 396307, 7, 7, 7),
    (7, 7, 7, 7, 332176, 7, 7, 7),
    (7, 7, 7, 7, 115074, 7, 7, 7),
    (7, 7, 7, 7, 61827, 7, 7, 7),
    (7, 7, 7, 7, 180614, 7, 7, 7),
    (7, 7, 7, 7, 317716, 7, 7, 7),
    (327088, 201462, 310480, 424721, 98851, 2327, 180630, 379156),
    (53282, 7, 127507, 371460, 176886, 339250, 359125, 53681),
    (82514, 7, 242182, 2391, 366933, 254966, 242550, 111011),
    (107075, 7, 400436, 7, 2359, 321941, 7, 254374),
    (311876, 7, 125989, 7, 7, 2391, 7, 181078),
    (299589, 7, 432401, 7, 7, 7, 7, 2359),
    (205382, 7, 321796, 7, 7, 7, 7, 209302),
    (7, 7, 321797, 7, 7, 7, 7, 7),
    (7, 7, 338228, 7, 7, 7, 7, 7),
    (7, 2359, 86659, 7, 344912, 326005, 7, 7),
    (7, 41810, 7, 7, 234310, 7, 7, 7),
    (7, 213830, 7, 7, 2583, 7, 7, 7),
    (74288, 314577, 2807, 110962, 7, 78225, 7, 7),
    (442913, 2327, 404565, 53603, 7, 237958, 7, 7),
    (213542, 7, 7, 205158, 7, 7, 7, 7),
    (217718, 7, 7, 259062, 7, 7, 7, 7),
    (323684, 180534, 429330, 181206, 334228, 70450, 330100, 2519),
    (221910, 314418, 102866, 2743, 338309, 242470, 338277, 397653),
    (7, 363445, 115139, 321940, 7, 189270, 2391, 168262),
    (7, 184886, 188870, 363760, 7, 7, 111570, 366996),
    (7, 70146, 318576, 7, 7, 7, 201670, 73731),
    (7, 338293, 343137, 7, 7, 7, 7, 2423),
    (7, 250358, 259062, 7, 7, 7, 7, 7),
    (7, 350613, 351060, 7, 7, 7, 7, 7),
    (7, 7, 90448, 7, 7, 7, 7, 7),
    (7, 7, 172358, 7, 7, 7, 7, 7),
    (7, 7, 351536, 7, 7, 7, 7, 7),
    (7, 7, 330929, 7, 7, 7, 7, 7),
    (7, 7, 2423, 7, 7, 7, 7, 7),
    (226038, 61872, 7, 70112, 115345, 2487, 2583, 330768),
    (351571, 197030, 7, 7, 123523, 342837, 119619, 338945),
    (7, 2519, 7, 7, 197254, 2519, 2455, 7),
    (7, 354805, 7, 7, 408626, 7, 7, 7),
    (7, 7, 7, 7, 2487, 7, 7, 7),
    (7, 7, 7, 7, 342516, 7, 7, 7),
    (7, 7, 7, 7, 334309, 7, 7, 7),
    (7, 7, 7, 7, 2519, 7, 7, 7),
    (72820, 94720, 387476, 78259, 365072, 193430, 197206, 7),
    (7, 7, 379269, 201126, 213510, 7, 342932, 7),
    (7, 7, 2679, 7, 354868, 7, 7, 7),
    (7, 7, 7, 7, 363045, 7, 7, 7),
    (359824, 259062, 192950, 432881, 7, 226166, 85013, 2487),
    (7, 2583, 424721, 346612, 7, 7, 7, 7),
    (7, 7, 375557, 2519, 7, 7, 7, 7),
    (353044, 7, 2519, 113937, 127857, 2647, 205334, 197206),
    (307973, 7, 209526, 7, 242534, 355440, 408144, 78323),
    (234246, 7, 379412, 7, 7, 363617, 371268, 246246),
    (7, 7, 371205, 7, 7, 217590, 2487, 2807),
    (7, 7, 225846, 7, 7, 246710, 371157, 226294),
    (7, 7, 7, 7, 7, 404016, 2871, 346900),
    (7, 7, 7, 7, 7, 363045, 2551, 358964),
    (359571, 238230, 2647, 246582, 221782, 2583, 107057, 86081),
    (98403, 209526, 7, 7, 82466, 230038, 254502, 2583),
    (327749, 2647, 7, 7, 2679, 2679, 221910, 119571),
    (7, 225974, 7, 7, 7, 7, 209526, 213766),
    (7, 7, 7, 99091, 2711, 375509, 7, 234358),
    (7, 7, 7, 221958, 7, 258806, 7, 7),
    (7, 7, 7, 367699, 7, 7, 7, 7),
    (7, 7, 7, 94768, 7, 7, 7, 7),
    (7, 7, 7, 225830, 7, 7, 7, 7),
    (238422, 2711, 7, 2647, 230070, 7, 412272, 102962),
    (365524, 2743, 7, 7, 7, 7, 375397, 205350),
    (345029, 234390, 7, 7, 7, 7, 383636, 399952),
    (246726, 7, 7, 7, 7, 7, 7, 375365),
    (7, 230102, 2711, 380208, 7, 371477, 387764, 259030),
    (7, 7, 7, 7, 7, 7, 383653, 2679),
    (7, 7, 7, 7, 7, 7, 250806, 217750),
    (81987, 379669, 230166, 238230, 2807, 117844, 384113, 7),
    (7, 7, 387765, 242358, 367412, 2903, 7, 7),
    (7, 7, 383701, 2775, 379685, 7, 7, 7),
    (364645, 2871, 416560, 7, 7, 7, 7, 7),
    (250742, 7, 7, 250742, 7, 2967, 2807, 2775),
    (90210, 7, 7, 375604, 7, 7, 7, 103155),
    (7, 7, 7, 7, 7, 7, 7, 242406),
    (7, 7, 7, 7, 7, 7, 7, 387892),
    (254870, 2967, 254806, 7, 238390, 2999, 2839, 2903),
    (7, 7, 384240, 7, 7, 7, 392337, 121909),
    (7, 7, 7, 7, 7, 7, 7, 2935),
    (7, 7, 7, 7, 7, 7, 7, 2967),
    (7, 7, 7, 2903, 7, 7, 7, 7),
    (7, 3031, 2935, 2935, 2935, 392148, 246582, 7),
    (7, 7, 7, 7, 7, 7, 2903, 7),
    (7, 7, 7, 7, 7, 7, 2935, 7),
    (259062, 7, 2967, 2967, 7, 7, 392368, 7),
    (7, 7, 2999, 7, 7, 7, 7, 7),
    (7, 7, 7, 7, 7, 7, 7, 2999),
    (7, 7, 392180, 7, 7, 7, 7, 7),
    (7, 7, 392165, 7, 7, 7, 7, 7),
    (7, 3063, 7, 2999, 254870, 3063, 392116, 3031),
    (7, 7, 7, 3031, 250806, 7, 388005, 3063),
    (7, 7, 7, 3063, 3063, 7, 3031, 7),
    (7, 7, 7, 7, 7, 7, 392181, 7),
)
SEGMENTS = (62, 8, 2, 6, 24, 9, 3, 4, 13, 8, 4, 3, 7, 4, 5, 4, 3, 3, 1, 0, 4, 2, 2, 1, 3, 2, 1, 2, 4, 0, 0, 0, 0)
BLOCKS = (
    (803072, 234697, 234570, 239723, 397952, 393901, 722030, 23951),
    (597068, 84289, 307395, 477344, 207824, 296586, 95593, 383079),
    (479365, 668590, 606657, 498284, 518885, 213059, 663765, 35152),
    (910961, 360727, 457207, 886943, 696792, 268111, 241674, 800914),
    (127290, 504977, 153151, 427560, 75679, 616151, 802669, 677733),
    (358443, 648028, 631450, 875248, 437373, 564604, 868543, 589065),
    (498359, 705315, 978648, 848856, 747361, 637821, 162359, 833372),
    (753085, 1039230, 943456, 972084, 249425, 1020888, 616339, 652510),
)
OWN = ((0, 4, 1, 1, 2, 14, 9, 4), (1, 0, 0, 0, 3, 0, 0, 0), (2, 16, 11, 9, 1, 1, 3, 2), (3, 25, 20, 15, 17, 24, 26, 22))
PARTNERS = ((0, 1, 1, 4, 2, 4, 9, 14), (1, 0, 0, 0, 3, 0, 0, 0), (2, 9, 11, 16, 1, 2, 3, 1), (3, 15, 20, 25, 17, 22, 26, 24))
MARKS = (10, 16, 19, 25, 32)
TRANSIT = 15
TI = 512

ROWS, COLS, RANK, HALF = 2048, 1024, 64, 1024
OTHER, COL_SLOT, TRANSIT_SLOT = 32, 64, 96
SLOTS = TRANSIT_SLOT + TRANSIT
NI = len(ITEMS)


def split(x):
    high = x.astype(BF16)
    return high, (x - high.astype(F32)).astype(BF16)


def kernel(
    trailing, factors, vectors, inverse, slots, out,
    acc, buf, right, wide, block_core, part, by_row, total, cores, known, table,
    local_sem, recv_sem, send_sem, own_send, row_send, row_recv, col_send, col_recv, out_sem,
):
    r, c = lax.axis_index("row"), lax.axis_index("col")
    z, x, y, k = r // 2, (r % 2) * 2 + (c // 2) % 2, c // 4, c % 2
    flip = x // 2
    sx, sy = 1 - 2 * flip, 1 - 2 * k
    xc = x + flip * (3 - 2 * x)
    delta = (sy * (y - z) + 4) % 4
    kind = xc * 4 + delta
    diagonal = jnp.where(kind == 0, 1, 0)
    q = c // 2

    def device(x, y, z, k):
        return (z * 2 + x // 2, y * 4 + (x % 2) * 2 + k)

    partner = (r, q * 2 + 1 - k)
    row_peers = [((r + i) % 8, c) for i in range(1, 8)]
    col_peers = [(r, (c + 2 * i) % 16) for i in range(1, 8)]
    outer = device(3 - x, y, z, k)

    start_acc = pltpu.make_async_copy(trailing, acc, local_sem.at[4])
    start_acc.start()
    bits = [kind % 2 == 1, (kind // 2) % 2 == 1, kind // 4 == 1]

    def pick(row):
        pairs = [jnp.where(bits[0], I32(row[2 * a + 1]), I32(row[2 * a])) for a in range(4)]
        pairs = [jnp.where(bits[1], pairs[2 * a + 1], pairs[2 * a]) for a in range(2)]
        return jnp.where(bits[2], pairs[1], pairs[0])

    own = []
    for j in range(2):
        here = jnp.where(k == 0, pick(OWN[j]), pick(OWN[2 + j]))
        there = jnp.where(k == 0, pick(PARTNERS[j]), pick(PARTNERS[2 + j]))
        for h in range(2):
            src = factors.at[pl.ds(j * RANK, RANK), pl.ds(h * HALF, HALF)]
            other = jnp.where(k == h, 0, 1)
            slot = here + OTHER * other
            own.append((src, there + OTHER * (1 - other)))
            pltpu.make_async_copy(src, buf.at[slot], recv_sem.at[slot]).start()

    barrier = pltpu.get_barrier_semaphore()
    greeted = row_peers + col_peers + [outer, partner]
    for peer in greeted:
        pl.semaphore_signal(barrier, inc=1, device_id=peer, device_id_type=MESH)

    for i, row in enumerate(ITEMS):
        table[i] = pick(row)

    nt = (((1,), (1,)), ((), ()))
    blank = jnp.zeros((RANK, RANK * 8), F32)
    first = lax.dot_general(
        vectors[0], jnp.concatenate([inverse[0], blank], axis=0), nt,
        precision=lax.Precision.HIGHEST, preferred_element_type=F32,
    )
    second = lax.dot_general(
        vectors[1], jnp.concatenate([blank, inverse[1]], axis=0), nt,
        precision=lax.Precision.HIGHEST, preferred_element_type=F32,
    )
    blank = jnp.zeros((RANK, 2 * RANK), F32)
    part[...] = lax.dot_general(
        first, jnp.concatenate([first, blank], axis=0), nt,
        precision=lax.Precision.HIGHEST, preferred_element_type=F32,
    ) + lax.dot_general(
        second, jnp.concatenate([blank, second], axis=0), nt,
        precision=lax.Precision.HIGHEST, preferred_element_type=F32,
    )
    block_core[...] = jnp.zeros_like(block_core)

    pl.semaphore_wait(barrier, len(greeted))

    own_copies = []
    for i, (src, slot) in enumerate(own):
        copy = pltpu.make_async_remote_copy(
            src_ref=src, dst_ref=buf.at[slot], send_sem=own_send.at[i], recv_sem=recv_sem.at[slot],
            device_id=partner, device_id_type=MESH,
        )
        copy.start()
        own_copies.append(copy)

    def arrived(slot):
        pltpu.make_async_copy(buf.at[slot], buf.at[slot], recv_sem.at[slot]).wait()

    def panel_at(code):
        block = 2 * ((sy * (code % 4) + z + 4) % 4) + (code // 4 + flip) % 2
        return 4 * block + code // 8

    def send_of(i, word):
        way = word % 16
        src, dst = (word // 32) % 128, (word // 4096) % 128
        axis, turn = way // 2, 1 - 2 * (way % 2)
        dx = jnp.where(axis == 0, sx * turn, 0)
        dy = jnp.where(axis == 1, sy * turn, 0)
        dz = jnp.where(axis == 2, sy * turn, 0)
        dk = jnp.where(axis == 3, 1, 0)
        target = device((x + dx + 4) % 4, (y + dy + 4) % 4, (z + dz + 4) % 4, (k + dk) % 2)
        return src, pltpu.make_async_remote_copy(
            src_ref=buf.at[src], dst_ref=buf.at[dst], send_sem=send_sem.at[i],
            recv_sem=recv_sem.at[dst], device_id=target, device_id_type=MESH,
        )

    def pass_on(i, word):
        src, copy = send_of(i, word)

        @pl.when((word // 16) % 2 == 1)
        def _():
            arrived(src)

        @pl.when(word % 16 < 7)
        def _():
            copy.start()

    def moves(i, _):
        pass_on(i, table[i])
        return 0

    def prepare(block):
        codes = pick(BLOCKS[block])
        for a in range(4):
            place = 4 * block + a
            arrived(OTHER + place)
            panel = panel_at((codes // (1 << (5 * a))) % 32)
            high, low = split(buf[jnp.where(diagonal == 1, place, COL_SLOT + place)])
            wide[pl.ds(a * RANK, RANK)] = high
            wide[pl.ds(256 + a * RANK, RANK)] = high
            wide[pl.ds(512 + a * RANK, RANK)] = low
            slot = slots[panel]
            pair = known[(slot // 2) % 2 * 8 + slot // 4]
            lane = lax.broadcasted_iota(I32, (RANK, 2 * RANK), 1) // RANK
            same = jnp.where(slot % 2 == a % 2, F32(1), F32(0))
            moved = pair * same + pltpu.roll(pair, RANK, axis=1) * (F32(1) - same)
            block_core[pl.ds(a * RANK, RANK), pl.ds((a // 2) * 128, 128)] = jnp.where(
                lane == a % 2, moved, F32(0)
            )
        high, low = split(block_core[...])
        scaled = jnp.dot(
            jnp.concatenate([high, low, high], axis=1), wide[...], preferred_element_type=F32
        )
        high, low = split(scaled)
        right[0:256] = high
        right[256:512] = high
        right[512:768] = low

    def tile_rows(j):
        h = k if j * TI < HALF else 1 - k
        return pl.ds(pl.multiple_of(h * HALF + (j * TI) % HALF, TI), TI)

    def store(j):
        return pltpu.make_async_copy(acc.at[tile_rows(j)], out.at[tile_rows(j)], out_sem.at[j])

    def tile(block, j):
        if j == 0:
            prepare(block)
        base = 4 * block + (0 if j * TI < HALF else OTHER)
        left = buf[base : base + 4, :, (j * TI) % HALF : (j * TI) % HALF + TI]
        high, low = split(left.reshape(256, TI))
        rows = tile_rows(j)
        acc[rows] = acc[rows] - lax.dot_general(
            jnp.concatenate([high, low, high], axis=0), right[...], (((0,), (0,)), ((), ())),
            preferred_element_type=F32,
        )
        if block == 7 and j > 0:
            store(j - 1).start()

    lax.fori_loop(0, MARKS[0], moves, 0)
    row_copies = []
    for i, peer in enumerate(row_peers):
        copy = pltpu.make_async_remote_copy(
            src_ref=part, dst_ref=by_row.at[7 - 1 - i], send_sem=row_send.at[i],
            recv_sem=row_recv.at[7 - 1 - i], device_id=peer, device_id_type=MESH,
        )
        copy.start()
        row_copies.append(copy)
    lax.fori_loop(MARKS[0], MARKS[1], moves, 0)
    for i in range(7):
        pltpu.make_async_copy(part, by_row.at[i], row_recv.at[i]).wait()
    summed = part[...]
    for i in range(7):
        summed = summed + by_row[i]
    total[...] = summed
    lax.fori_loop(MARKS[1], MARKS[2], moves, 0)
    mine = k * 8 + q
    keep = pltpu.make_async_copy(total, cores.at[mine], local_sem.at[5])
    keep.start()
    col_copies = []
    for i, peer in enumerate(col_peers):
        copy = pltpu.make_async_remote_copy(
            src_ref=total, dst_ref=cores.at[mine], send_sem=col_send.at[i],
            recv_sem=col_recv.at[i], device_id=peer, device_id_type=MESH,
        )
        copy.start()
        col_copies.append(copy)
    lax.fori_loop(MARKS[2], MARKS[3], moves, 0)
    keep.wait()
    for i in range(7):
        sender = k * 8 + (q + 7 - i) % 8
        pltpu.make_async_copy(total, cores.at[sender], col_recv.at[i]).wait()
    half = cores.at[pl.ds(k * 8, 8)]
    exchange = pltpu.make_async_remote_copy(
        src_ref=half, dst_ref=half, send_sem=col_send.at[7], recv_sem=col_recv.at[7],
        device_id=partner, device_id_type=MESH,
    )
    exchange.start()
    lax.fori_loop(MARKS[3], MARKS[4], moves, 0)
    exchange.wait_recv()
    settle = pltpu.make_async_copy(cores, known, local_sem.at[6])
    settle.start()
    settle.wait()
    start_acc.wait()
    tiles = ROWS // TI
    done = MARKS[4]
    end = 0
    for t, length in enumerate(SEGMENTS):
        end += length
        if end > done:
            lax.fori_loop(done, end, moves, 0)
            done = end
        if t < 8 * tiles:
            tile(t // tiles, t % tiles)
    store(tiles - 1).start()

    for copy in own_copies + row_copies + col_copies + [exchange]:
        copy.wait_send()

    def sent(i, _):
        word = table[i]

        @pl.when(word % 16 < 7)
        def _():
            send_of(i, word)[1].wait_send()

        return 0

    lax.fori_loop(0, NI, sent, 0)
    for t in range(ROWS // TI):
        store(t).wait()


def body(trailing, panel_factors, vectors_t, inverse_lower_factors, slot_of_panel):
    hbm = pl.BlockSpec(memory_space=pl.ANY)
    vmem = pl.BlockSpec(memory_space=pltpu.VMEM)
    dma = pltpu.SemaphoreType.DMA
    return pl.pallas_call(
        kernel,
        out_shape=jax.ShapeDtypeStruct((ROWS, COLS), F32),
        in_specs=[hbm, hbm, vmem, vmem, pl.BlockSpec(memory_space=pltpu.SMEM)],
        out_specs=hbm,
        scratch_shapes=[
            pltpu.VMEM((ROWS, COLS), F32),
            pltpu.VMEM((SLOTS, RANK, HALF), F32),
            pltpu.VMEM((768, COLS), BF16),
            pltpu.VMEM((768, COLS), BF16),
            pltpu.VMEM((256, 256), F32),
            pltpu.VMEM((RANK, 2 * RANK), F32),
            pltpu.VMEM((7, RANK, 2 * RANK), F32),
            pltpu.VMEM((RANK, 2 * RANK), F32),
            pltpu.VMEM((16, RANK, 2 * RANK), F32),
            pltpu.VMEM((16, RANK, 2 * RANK), F32),
            pltpu.SMEM((NI,), I32),
            dma((7,)), dma((SLOTS,)), dma((NI,)), dma((4,)), dma((7,)), dma((7,)), dma((8,)), dma((8,)),
            dma((ROWS // TI,)),
        ],
        compiler_params=pltpu.CompilerParams(
            collective_id=0, has_side_effects=True, vmem_limit_bytes=56 * 2**20
        ),
        name="update",
    )(trailing, panel_factors, vectors_t, inverse_lower_factors, slot_of_panel)


def solution(mesh):
    return jax.shard_map(
        body,
        mesh=mesh,
        in_specs=(
            P("row", "col"),
            P("col", "row"),
            P("col", None, None),
            P("col", "row", None),
            P(),
        ),
        out_specs=P("row", "col"),
        check_vma=False,
    )
```

```python
import jax
import jax.numpy as jnp
from jax import lax
from jax.experimental import pallas as pl
from jax.experimental.pallas import tpu as pltpu
from jax.sharding import PartitionSpec as P

MESH = pl.DeviceIdType.MESH
F32, BF16, I32 = jnp.float32, jnp.bfloat16, jnp.int32

ITEMS = (
    (9, 9, 9, 9, 9, 9, 9, 9),
    (8243, 16592, 33040, 29042, 17265, 438800, 422256, 16883),
    (127088, 10, 4274, 77939, 4947, 29233, 107249, 397909),
    (450641, 24691, 10, 393237, 10, 90659, 37219, 10),
    (262213, 11, 77875, 10, 20529, 10, 10, 421904),
    (10, 95059, 11, 28768, 111458, 57890, 25314, 53825),
    (94227, 102642, 69648, 74387, 11, 61555, 11, 11),
    (11, 397541, 32771, 11, 21314, 11, 98322, 16433),
    (262244, 209126, 49776, 12643, 408626, 53762, 16529, 401445),
    (16386, 264213, 160358, 401493, 70353, 273779, 401541, 151590),
    (12528, 8290, 4259, 139334, 213702, 393364, 188550, 110707),
    (463073, 77843, 238422, 16432, 86051, 159878, 412913, 123089),
    (266468, 107120, 306227, 135206, 263152, 442672, 33042, 69874),
    (155878, 201318, 20738, 268308, 54242, 82209, 86275, 37058),
    (359442, 28866, 393813, 119218, 95203, 24867, 164102, 147686),
    (65600, 37059, 188998, 24995, 259046, 168230, 410068, 159942),
    (8226, 12, 12, 430501, 303600, 430960, 147910, 400467),
    (37011, 409876, 49970, 180646, 209382, 21345, 102514, 310514),
    (147590, 188678, 148262, 90864, 41793, 66402, 12, 429284),
    (269776, 45200, 77970, 398053, 12, 140134, 66417, 12),
    (8400, 422020, 53379, 148198, 396307, 12, 123747, 16530),
    (270532, 225414, 233606, 12, 333908, 282003, 217958, 135302),
    (266437, 205462, 440337, 119424, 416850, 110609, 123442, 418576),
    (159942, 13, 13, 32866, 139382, 404626, 8739, 41729),
    (277586, 419889, 4208, 272436, 13, 388403, 201254, 33538),
    (12, 276517, 65635, 13, 264212, 429348, 322834, 221958),
    (54000, 4144, 139366, 396307, 264197, 13, 453891, 406197),
    (459489, 45091, 2103, 69779, 344624, 21171, 13, 225958),
    (221926, 405540, 8272, 254086, 180774, 164518, 37297, 13),
    (446641, 135206, 24642, 434485, 53457, 426160, 49570, 268852),
    (118946, 412401, 143430, 151846, 155846, 123041, 168358, 294098),
    (28835, 309989, 272468, 49330, 9059, 106658, 94305, 176854),
    (151718, 53426, 57346, 221350, 119314, 135334, 29411, 217366),
    (339504, 442532, 113809, 415825, 20995, 69729, 416816, 99059),
    (286002, 168102, 168150, 114688, 197126, 459600, 76836, 185062),
    (13, 280917, 277872, 62418, 420978, 119618, 82323, 426928),
    (41584, 49234, 2167, 172998, 285012, 29507, 151942, 103330),
    (352868, 426052, 7, 114931, 272709, 189254, 197142, 164774),
    (295525, 139334, 7, 438501, 65553, 238550, 411696, 264212),
    (205414, 302288, 7, 250086, 306451, 326768, 268324, 115506),
    (7, 2135, 7, 184726, 282928, 76900, 41010, 230182),
    (7, 32768, 7, 338644, 168230, 40962, 24611, 77922),
    (7, 45890, 7, 273584, 288917, 82290, 139302, 269328),
    (7, 127859, 7, 123219, 276532, 425236, 420944, 115603),
    (7, 416019, 7, 176454, 276517, 221542, 68677, 234374),
    (7, 246630, 7, 160374, 49746, 197206, 416949, 403633),
    (7, 284789, 7, 346612, 188998, 86114, 230166, 86994),
    (7, 306320, 7, 428593, 289428, 298515, 37218, 140230),
    (7, 7, 7, 2231, 285317, 433668, 238422, 409680),
    (7, 7, 7, 53456, 40962, 2071, 2071, 241734),
    (7, 7, 7, 196806, 2423, 254038, 135254, 343314),
    (7, 7, 7, 293969, 294131, 225718, 58290, 205334),
    (7, 7, 7, 322611, 45059, 147510, 250790, 285875),
    (7, 7, 7, 432241, 3031, 2103, 289937, 280628),
    (7, 7, 7, 297060, 319568, 276980, 280661, 408017),
    (7, 7, 7, 74370, 143430, 272869, 90449, 338372),
    (7, 7, 7, 350484, 343347, 434720, 160070, 114689),
    (7, 7, 7, 363792, 346292, 403537, 78739, 123059),
    (7, 7, 7, 7, 346277, 325701, 205702, 250022),
    (7, 7, 7, 7, 286864, 433621, 2167, 2135),
    (7, 7, 7, 7, 147590, 281776, 457940, 2167),
    (7, 7, 7, 7, 299184, 294049, 2551, 7),
    (7, 7, 7, 7, 151718, 98307, 7, 7),
    (7, 7, 7, 7, 2167, 301365, 7, 7),
    (7, 7, 7, 7, 7, 288981, 7, 7),
    (7, 7, 7, 7, 7, 314707, 7, 7),
    (7, 7, 7, 7, 7, 127250, 7, 7),
    (7, 7, 7, 7, 7, 250118, 7, 7),
    (7, 7, 7, 7, 7, 41201, 7, 7),
    (7, 7, 7, 7, 7, 155878, 7, 7),
    (7, 7, 7, 7, 7, 152502, 7, 7),
    (7, 7, 7, 7, 7, 57859, 7, 7),
    (7, 7, 7, 7, 7, 49665, 7, 7),
    (7, 7, 7, 7, 7, 297109, 7, 7),
    (7, 7, 7, 7, 7, 314866, 7, 7),
    (7, 7, 7, 7, 7, 2167, 7, 7),
    (246710, 57779, 20720, 86482, 176566, 395600, 7, 37443),
    (188982, 180646, 32994, 418245, 7, 358724, 7, 2199),
    (7, 148438, 209126, 164294, 7, 305477, 7, 7),
    (7, 355568, 334197, 2199, 7, 213654, 7, 7),
    (7, 343265, 119314, 40963, 7, 298192, 7, 7),
    (7, 445669, 250374, 7, 7, 7, 7, 7),
    (289842, 160694, 90371, 306289, 82193, 321717, 7, 421013),
    (326803, 119346, 76820, 310480, 164102, 7, 7, 7),
    (364048, 107043, 400389, 371905, 2519, 7, 7, 7),
    (425477, 250406, 242550, 313556, 7, 7, 7, 7),
    (7, 7, 7, 90114, 7, 7, 7, 7),
    (7, 7, 7, 317972, 7, 7, 7, 7),
    (49456, 156182, 280725, 168214, 159990, 7, 180406, 65937),
    (454945, 7, 7, 2295, 7, 7, 32048, 180614),
    (164134, 7, 7, 7, 7, 7, 395408, 436563),
    (37138, 7, 7, 7, 7, 7, 292996, 156086),
    (282884, 7, 7, 7, 7, 7, 213654, 2263),
    (278789, 7, 7, 7, 7, 7, 407728, 7),
    (168198, 7, 7, 7, 7, 7, 309412, 7),
    (7, 7, 7, 7, 7, 7, 297125, 7),
    (172374, 293013, 184758, 7, 301652, 184534, 69842, 188758),
    (7, 301237, 155958, 7, 313556, 48148, 61635, 411889),
    (7, 57440, 2647, 7, 313541, 61841, 155846, 383205),
    (7, 115280, 201270, 7, 342261, 180614, 408145, 2711),
    (7, 193094, 436401, 7, 322770, 2775, 318020, 7),
    (7, 322641, 24976, 7, 7, 2295, 107186, 7),
    (7, 420933, 180614, 7, 7, 7, 242342, 7),
    (7, 2679, 103154, 7, 7, 7, 254934, 7),
    (7, 152278, 58083, 7, 7, 7, 2359, 7),
    (7, 2359, 226022, 7, 7, 7, 317653, 7),
    (7, 415953, 424593, 7, 7, 7, 127219, 7),
    (7, 2295, 294288, 7, 7, 7, 172262, 7),
    (7, 7, 306561, 7, 7, 7, 98403, 7),
    (7, 7, 421253, 7, 7, 7, 416017, 7),
    (7, 7, 246678, 7, 7, 7, 193526, 7),
    (7, 7, 310608, 7, 7, 7, 184630, 7),
    (7, 7, 127346, 7, 7, 7, 2295, 7),
    (7, 7, 172390, 7, 7, 7, 7, 7),
    (7, 7, 69666, 7, 7, 7, 7, 7),
    (7, 7, 346324, 7, 7, 7, 7, 7),
    (7, 7, 301253, 7, 7, 7, 7, 7),
    (7, 7, 2295, 7, 7, 7, 7, 7),
    (314706, 233942, 46035, 62355, 2327, 334101, 343057, 2839),
    (396530, 2519, 254918, 242566, 323920, 346773, 7, 94210),
    (277731, 2551, 355568, 201654, 233798, 172502, 7, 7),
    (331184, 164150, 99250, 403891, 7, 258678, 7, 7),
    (176502, 7, 197542, 326324, 7, 115025, 7, 7),
    (295316, 7, 2327, 326960, 7, 414020, 7, 7),
    (299397, 7, 7, 2359, 7, 176454, 7, 7),
    (180614, 7, 7, 7, 7, 7, 7, 7),
    (328116, 7, 111314, 7, 330036, 403824, 2391, 7),
    (324005, 7, 193222, 7, 338213, 334180, 7, 7),
    (184742, 7, 338229, 7, 172854, 7, 7, 7),
    (7, 7, 432593, 7, 7, 7, 7, 7),
    (7, 7, 350660, 7, 7, 7, 7, 7),
    (7, 7, 321989, 7, 7, 7, 7, 7),
    (335218, 254294, 102560, 7, 2807, 7, 330100, 317748),
    (289907, 7, 7, 7, 7, 7, 338277, 74033),
    (355824, 7, 7, 7, 7, 7, 350612, 168230),
    (7, 7, 7, 7, 7, 7, 354693, 86385),
    (7, 7, 7, 7, 7, 7, 449876, 78179),
    (7, 7, 7, 7, 7, 7, 7, 409957),
    (7, 7, 7, 7, 7, 7, 7, 172390),
    (7, 7, 7, 7, 7, 7, 7, 2327),
    (7, 7, 7, 7, 7, 7, 7, 2423),
    (349172, 103232, 127315, 2391, 316176, 62354, 375220, 330132),
    (308197, 335024, 176454, 193046, 78595, 2455, 7, 7),
    (254950, 2711, 2743, 189238, 226054, 242566, 7, 7),
    (7, 2423, 2391, 2423, 94242, 7, 7, 7),
    (7, 172406, 330961, 7, 2839, 7, 7, 7),
    (7, 2455, 355441, 7, 2999, 7, 7, 7),
    (7, 7, 330132, 7, 184694, 7, 7, 7),
    (7, 7, 7, 7, 349072, 7, 7, 7),
    (7, 7, 7, 7, 99201, 7, 7, 7),
    (7, 7, 7, 7, 246662, 7, 7, 7),
    (311796, 184726, 98803, 2647, 350708, 201206, 367729, 238038),
    (315877, 57346, 221670, 2455, 362981, 2487, 209526, 342644),
    (192998, 408241, 351536, 2903, 2455, 85076, 2519, 2487),
    (318867, 7, 7, 127984, 82323, 2519, 90115, 358900),
    (197142, 7, 7, 259046, 201094, 74546, 387796, 7),
    (64692, 7, 7, 343185, 7, 246566, 371397, 7),
    (310547, 7, 7, 424401, 7, 363125, 258550, 7),
    (7, 334261, 2487, 82643, 7, 7, 7, 7),
    (7, 89109, 7, 217798, 7, 7, 7, 7),
    (7, 7, 7, 111088, 7, 7, 7, 7),
    (7, 7, 7, 205286, 7, 7, 7, 7),
    (201174, 259062, 400468, 7, 425106, 7, 7, 371220),
    (7, 7, 371889, 7, 365168, 7, 7, 193078),
    (7, 7, 7, 7, 103009, 7, 7, 258678),
    (7, 7, 7, 7, 193126, 7, 7, 7),
    (7, 7, 7, 7, 408755, 7, 7, 7),
    (7, 7, 7, 7, 358836, 7, 7, 7),
    (7, 7, 7, 7, 371109, 7, 7, 7),
    (234326, 197110, 205270, 7, 115153, 209910, 2583, 7),
    (7, 359536, 2551, 7, 205254, 90866, 383541, 7),
    (7, 7, 7, 7, 377520, 217830, 246358, 7),
    (7, 7, 7, 7, 217766, 7, 7, 7),
    (209494, 363285, 2583, 111154, 2583, 399920, 234294, 399952),
    (90179, 2583, 2615, 209446, 2615, 371236, 7, 375365),
    (339154, 358965, 354932, 213590, 221846, 2583, 7, 209910),
    (361109, 7, 359013, 127827, 375476, 2647, 7, 7),
    (213638, 7, 213654, 226118, 379557, 234262, 7, 7),
    (217782, 7, 217782, 2679, 2679, 7, 7, 7),
    (7, 7, 7, 367856, 7, 7, 7, 7),
    (7, 7, 7, 2711, 7, 7, 7, 7),
    (7, 7, 7, 234262, 7, 7, 7, 7),
    (7, 7, 7, 246454, 7, 7, 7, 7),
    (7, 99218, 7, 7, 7, 367856, 428657, 254806),
    (7, 217990, 7, 7, 7, 376033, 391780, 213654),
    (7, 7, 7, 7, 7, 7, 221910, 7),
    (7, 242454, 379604, 7, 123633, 230102, 2711, 2743),
    (7, 375858, 375573, 7, 230118, 2743, 7, 7),
    (7, 7, 7, 7, 2775, 7, 7, 7),
    (226006, 2647, 230166, 230262, 7, 2807, 7, 7),
    (7, 221878, 7, 7, 7, 375573, 7, 7),
    (7, 7, 7, 7, 7, 121908, 7, 7),
    (7, 379701, 383733, 2839, 387892, 368050, 2743, 246646),
    (7, 7, 387892, 7, 383781, 7, 2807, 380016),
    (7, 7, 387877, 7, 7, 7, 7, 380001),
    (7, 7, 7, 7, 7, 7, 7, 2775),
    (106595, 238326, 2903, 2807, 2903, 7, 391957, 2807),
    (7, 2775, 7, 7, 2935, 7, 7, 126005),
    (7, 230198, 259062, 7, 7, 2871, 7, 2871),
    (7, 7, 2935, 7, 7, 379733, 7, 7),
    (86082, 7, 7, 383796, 7, 7, 7, 7),
    (344132, 387957, 2967, 2935, 2967, 7, 2871, 2903),
    (7, 2903, 7, 7, 250806, 7, 2903, 383892),
    (7, 2967, 7, 7, 7, 7, 2935, 392069),
    (7, 7, 7, 7, 7, 7, 7, 2935),
    (7, 2999, 392465, 2967, 254934, 2935, 7, 7),
    (7, 7, 7, 7, 7, 387989, 7, 7),
    (361236, 7, 7, 7, 7, 7, 7, 7),
    (365317, 7, 7, 7, 7, 7, 7, 7),
    (230150, 7, 7, 7, 7, 7, 7, 7),
    (368741, 7, 7, 7, 7, 7, 7, 2999),
    (94306, 7, 7, 7, 7, 7, 7, 7),
    (103218, 7, 7, 7, 7, 7, 7, 7),
    (365348, 7, 7, 7, 7, 7, 7, 7),
    (381733, 7, 7, 7, 7, 7, 7, 7),
    (238374, 7, 7, 7, 7, 7, 7, 7),
    (242550, 7, 7, 7, 7, 7, 7, 7),
    (250774, 7, 7, 7, 7, 7, 7, 7),
    (7, 3031, 2999, 2999, 7, 392117, 2967, 3031),
    (7, 7, 7, 7, 7, 3031, 2999, 7),
    (7, 7, 3031, 7, 3063, 7, 7, 7),
    (7, 7, 392180, 3031, 7, 3063, 3031, 3063),
    (7, 7, 392165, 7, 7, 7, 7, 7),
    (259030, 3063, 7, 3063, 7, 7, 3063, 7),
)
SEGMENTS = (76, 6, 6, 8, 22, 8, 6, 9, 10, 7, 4, 7, 4, 10, 3, 3, 3, 4, 2, 2, 1, 4, 2, 3, 8, 2, 1, 2, 1, 0, 0, 0, 0)
BLOCKS = (
    (803072, 303441, 370514, 106843, 370332, 706909, 730494, 766111),
    (370316, 165248, 48455, 664644, 866378, 208001, 1024039, 104970),
    (331811, 989298, 847266, 391553, 902366, 29137, 488930, 929218),
    (204226, 514285, 1033608, 575973, 702241, 272143, 628131, 256301),
    (576700, 872107, 117911, 244557, 769136, 892077, 943692, 965893),
    (847454, 789006, 750608, 17299, 1021511, 686147, 217760, 787073),
    (874230, 976639, 465084, 975573, 397949, 420662, 758104, 579294),
    (982509, 889500, 817844, 826111, 794646, 1039891, 574299, 838267),
)
OWN = ((0, 6, 8, 3, 26, 17, 23, 15), (1, 3, 5, 11, 27, 16, 11, 18), (2, 0, 0, 20, 1, 3, 3, 3), (3, 26, 1, 0, 0, 0, 0, 0))
PARTNERS = ((0, 3, 8, 6, 26, 15, 23, 17), (1, 11, 5, 3, 27, 18, 11, 16), (2, 20, 0, 0, 1, 3, 3, 3), (3, 0, 1, 26, 0, 0, 0, 0))
TRANSIT = 18
TI = 512

ROWS, COLS, RANK, HALF = 2048, 1024, 64, 1024
OTHER, COL_SLOT, TRANSIT_SLOT = 32, 64, 96
SLOTS = TRANSIT_SLOT + TRANSIT
NI = len(ITEMS)


def split(x):
    high = x.astype(BF16)
    return high, (x - high.astype(F32)).astype(BF16)


def kernel(
    trailing, factors, vectors, inverse, slots, acc,
    buf, right, wide, block_core, part, by_row, total, cores, known, table,
    local_sem, recv_sem, send_sem, own_send, row_send, row_recv, col_send, col_recv,
):
    r, c = lax.axis_index("row"), lax.axis_index("col")
    z, x, y, k = r // 2, (r % 2) * 2 + (c // 2) % 2, c // 4, c % 2
    flip = x // 2
    sx, sy = 1 - 2 * flip, 1 - 2 * k
    xc = x + flip * (3 - 2 * x)
    delta = (sy * (y - z) + 4) % 4
    kind = xc * 4 + delta
    diagonal = jnp.where(kind == 0, 1, 0)
    q = c // 2

    def device(x, y, z, k):
        return (z * 2 + x // 2, y * 4 + (x % 2) * 2 + k)

    partner = (r, q * 2 + 1 - k)
    row_peers = [((r + i) % 8, c) for i in range(1, 8)]
    col_peers = [(r, (c + 2 * i) % 16) for i in range(1, 8)]
    outer = device(3 - x, y, z, k)

    start_acc = pltpu.make_async_copy(trailing, acc, local_sem.at[4])
    start_acc.start()
    bits = [kind % 2 == 1, (kind // 2) % 2 == 1, kind // 4 == 1]

    def pick(row):
        pairs = [jnp.where(bits[0], I32(row[2 * a + 1]), I32(row[2 * a])) for a in range(4)]
        pairs = [jnp.where(bits[1], pairs[2 * a + 1], pairs[2 * a]) for a in range(2)]
        return jnp.where(bits[2], pairs[1], pairs[0])

    own = []
    for j in range(2):
        here = jnp.where(k == 0, pick(OWN[j]), pick(OWN[2 + j]))
        there = jnp.where(k == 0, pick(PARTNERS[j]), pick(PARTNERS[2 + j]))
        for h in range(2):
            src = factors.at[pl.ds(j * RANK, RANK), pl.ds(h * HALF, HALF)]
            other = jnp.where(k == h, 0, 1)
            slot = here + OTHER * other
            own.append((src, there + OTHER * (1 - other)))
            pltpu.make_async_copy(src, buf.at[slot], recv_sem.at[slot]).start()

    barrier = pltpu.get_barrier_semaphore()
    greeted = row_peers + col_peers + [outer, partner]
    for peer in greeted:
        pl.semaphore_signal(barrier, inc=1, device_id=peer, device_id_type=MESH)

    for i, row in enumerate(ITEMS):
        table[i] = pick(row)

    nt = (((1,), (1,)), ((), ()))
    blank = jnp.zeros((RANK, RANK * 8), F32)
    first = lax.dot_general(
        vectors[0], jnp.concatenate([inverse[0], blank], axis=0), nt,
        precision=lax.Precision.HIGHEST, preferred_element_type=F32,
    )
    second = lax.dot_general(
        vectors[1], jnp.concatenate([blank, inverse[1]], axis=0), nt,
        precision=lax.Precision.HIGHEST, preferred_element_type=F32,
    )
    blank = jnp.zeros((RANK, 2 * RANK), F32)
    part[...] = lax.dot_general(
        first, jnp.concatenate([first, blank], axis=0), nt,
        precision=lax.Precision.HIGHEST, preferred_element_type=F32,
    ) + lax.dot_general(
        second, jnp.concatenate([blank, second], axis=0), nt,
        precision=lax.Precision.HIGHEST, preferred_element_type=F32,
    )
    block_core[...] = jnp.zeros_like(block_core)

    pl.semaphore_wait(barrier, len(greeted))

    own_copies = []
    for i, (src, slot) in enumerate(own):
        copy = pltpu.make_async_remote_copy(
            src_ref=src, dst_ref=buf.at[slot], send_sem=own_send.at[i], recv_sem=recv_sem.at[slot],
            device_id=partner, device_id_type=MESH,
        )
        copy.start()
        own_copies.append(copy)

    def arrived(slot):
        pltpu.make_async_copy(buf.at[slot], buf.at[slot], recv_sem.at[slot]).wait()

    def panel_at(code):
        block = 2 * ((sy * (code % 4) + z + 4) % 4) + (code // 4 + flip) % 2
        return 4 * block + code // 8

    def send_of(i, word):
        way = word % 16
        src, dst = (word // 32) % 128, (word // 4096) % 128
        axis, turn = way // 2, 1 - 2 * (way % 2)
        dx = jnp.where(axis == 0, sx * turn, 0)
        dy = jnp.where(axis == 1, sy * turn, 0)
        dz = jnp.where(axis == 2, sy * turn, 0)
        dk = jnp.where(axis == 3, 1, 0)
        target = device((x + dx + 4) % 4, (y + dy + 4) % 4, (z + dz + 4) % 4, (k + dk) % 2)
        return src, pltpu.make_async_remote_copy(
            src_ref=buf.at[src], dst_ref=buf.at[dst], send_sem=send_sem.at[i],
            recv_sem=recv_sem.at[dst], device_id=target, device_id_type=MESH,
        )

    def pass_on(i, word):
        src, copy = send_of(i, word)

        @pl.when((word // 16) % 2 == 1)
        def _():
            arrived(src)

        @pl.when(word % 16 < 7)
        def _():
            copy.start()

    def moves(i, _):
        pass_on(i, table[i])
        return 0

    def sent(i, _):
        @pl.when(table[i] % 16 < 7)
        def _():
            pltpu.make_async_copy(buf.at[0], buf.at[0], send_sem.at[i]).wait()

        return 0

    def prepare(block):
        codes = pick(BLOCKS[block])
        for a in range(4):
            place = 4 * block + a
            arrived(OTHER + place)
            panel = panel_at((codes // (1 << (5 * a))) % 32)
            high, low = split(buf[jnp.where(diagonal == 1, place, COL_SLOT + place)])
            wide[pl.ds(a * RANK, RANK)] = high
            wide[pl.ds(256 + a * RANK, RANK)] = high
            wide[pl.ds(512 + a * RANK, RANK)] = low
            slot = slots[panel]
            pair = known[(slot // 2) % 2 * 8 + slot // 4]
            lane = lax.broadcasted_iota(I32, (RANK, 2 * RANK), 1) // RANK
            same = jnp.where(slot % 2 == a % 2, F32(1), F32(0))
            moved = pair * same + pltpu.roll(pair, RANK, axis=1) * (F32(1) - same)
            block_core[pl.ds(a * RANK, RANK), pl.ds((a // 2) * 128, 128)] = jnp.where(
                lane == a % 2, moved, F32(0)
            )
        high, low = split(block_core[...])
        scaled = jnp.dot(
            jnp.concatenate([high, low, high], axis=1), wide[...], preferred_element_type=F32
        )
        high, low = split(scaled)
        right[0:256] = high
        right[256:512] = high
        right[512:768] = low

    def tile_rows(j):
        h = k if j * TI < HALF else 1 - k
        return pl.ds(pl.multiple_of(h * HALF + (j * TI) % HALF, TI), TI)

    def tile(block, j):
        if j == 0:
            prepare(block)
        base = 4 * block + (0 if j * TI < HALF else OTHER)
        left = buf[base : base + 4, :, (j * TI) % HALF : (j * TI) % HALF + TI]
        high, low = split(left.reshape(256, TI))
        rows = tile_rows(j)
        acc[rows] = acc[rows] - lax.dot_general(
            jnp.concatenate([high, low, high], axis=0), right[...], (((0,), (0,)), ((), ())),
            preferred_element_type=F32,
        )

    mine = k * 8 + q
    row_copies = [
        pltpu.make_async_remote_copy(
            src_ref=part, dst_ref=by_row.at[6 - i], send_sem=row_send.at[i],
            recv_sem=row_recv.at[6 - i], device_id=peer, device_id_type=MESH,
        )
        for i, peer in enumerate(row_peers)
    ]
    keep = pltpu.make_async_copy(total, cores.at[mine], local_sem.at[5])
    col_copies = [
        pltpu.make_async_remote_copy(
            src_ref=total, dst_ref=cores.at[mine], send_sem=col_send.at[i],
            recv_sem=col_recv.at[i], device_id=peer, device_id_type=MESH,
        )
        for i, peer in enumerate(col_peers)
    ]
    half = cores.at[pl.ds(k * 8, 8)]
    exchange = pltpu.make_async_remote_copy(
        src_ref=half, dst_ref=half, send_sem=col_send.at[7], recv_sem=col_recv.at[7],
        device_id=partner, device_id_type=MESH,
    )
    settle = pltpu.make_async_copy(cores, known, local_sem.at[6])

    def give_share():
        for copy in row_copies:
            copy.start()

    def add_shares():
        for i in range(7):
            pltpu.make_async_copy(part, by_row.at[i], row_recv.at[i]).wait()
        summed = part[...]
        for i in range(7):
            summed = summed + by_row[i]
        total[...] = summed

    def give_total():
        keep.start()
        for copy in col_copies:
            copy.start()

    def give_half():
        keep.wait()
        for i in range(7):
            sender = k * 8 + (q + 7 - i) % 8
            pltpu.make_async_copy(total, cores.at[sender], col_recv.at[i]).wait()
        exchange.start()

    def take_half():
        exchange.wait_recv()
        settle.start()
        settle.wait()
        start_acc.wait()

    def opening(i, _):
        word = table[i]

        @pl.when(word % 16 < 8)
        def _():
            pass_on(i, word)

        for phase, action in enumerate((give_share, add_shares, give_total, give_half, take_half)):
            pl.when(word % 16 == 9 + phase)(action)
        return 0

    lax.fori_loop(0, SEGMENTS[0], opening, 0)
    tiles = ROWS // TI
    done = SEGMENTS[0]
    end = checked = 0
    for t, length in enumerate(SEGMENTS):
        end += length
        if end > done:
            lax.fori_loop(done, end, moves, 0)
            done = end
        if t in (4 * tiles, 7 * tiles):
            early = sum(SEGMENTS[: t - tiles])
            lax.fori_loop(checked, early, sent, 0)
            checked = early
        if t < 8 * tiles:
            tile(t // tiles, t % tiles)

    for copy in own_copies + row_copies + col_copies + [exchange]:
        copy.wait_send()

    lax.fori_loop(checked, NI, sent, 0)


def body(trailing, panel_factors, vectors_t, inverse_lower_factors, slot_of_panel):
    hbm = pl.BlockSpec(memory_space=pl.ANY)
    vmem = pl.BlockSpec(memory_space=pltpu.VMEM)
    dma = pltpu.SemaphoreType.DMA
    return pl.pallas_call(
        kernel,
        out_shape=pltpu.VMEM((ROWS, COLS), F32),
        in_specs=[hbm, hbm, vmem, vmem, pl.BlockSpec(memory_space=pltpu.SMEM)],
        out_specs=vmem,
        scratch_shapes=[
            pltpu.VMEM((SLOTS, RANK, HALF), F32),
            pltpu.VMEM((768, COLS), BF16),
            pltpu.VMEM((768, COLS), BF16),
            pltpu.VMEM((256, 256), F32),
            pltpu.VMEM((RANK, 2 * RANK), F32),
            pltpu.VMEM((7, RANK, 2 * RANK), F32),
            pltpu.VMEM((RANK, 2 * RANK), F32),
            pltpu.VMEM((16, RANK, 2 * RANK), F32),
            pltpu.VMEM((16, RANK, 2 * RANK), F32),
            pltpu.SMEM((NI,), I32),
            dma((7,)), dma((SLOTS,)), dma((NI,)), dma((4,)), dma((7,)), dma((7,)), dma((8,)), dma((8,)),
        ],
        compiler_params=pltpu.CompilerParams(
            collective_id=0, has_side_effects=True, vmem_limit_bytes=55 * 2**20
        ),
        name="update",
    )(trailing, panel_factors, vectors_t, inverse_lower_factors, slot_of_panel)


def solution(mesh):
    return jax.shard_map(
        body,
        mesh=mesh,
        in_specs=(
            P("row", "col"),
            P("col", "row"),
            P("col", None, None),
            P("col", "row", None),
            P(),
        ),
        out_specs=P("row", "col"),
        check_vma=False,
    )
```

```python
import jax
import jax.numpy as jnp
from jax import lax
from jax.experimental import pallas as pl
from jax.experimental.pallas import tpu as pltpu
from jax.sharding import PartitionSpec as P

MESH = pl.DeviceIdType.MESH
F32, BF16, I32 = jnp.float32, jnp.bfloat16, jnp.int32

ITEMS = (
    (9, 9, 9, 9, 9, 9, 9, 9),
    (8240, 24754, 16, 24656, 16497, 430096, 20561, 61489),
    (458769, 397476, 33106, 426049, 24674, 45426, 41267, 393397),
    (36866, 10, 10, 36914, 413748, 78179, 10, 10),
    (262181, 57392, 4144, 10, 262288, 10, 102609, 430192),
    (10, 74227, 20482, 86051, 10, 107057, 90179, 65634),
    (3, 11, 11, 394069, 29107, 11, 11, 49251),
    (266325, 12304, 58098, 11, 413733, 401956, 45250, 397813),
    (11, 8496, 28882, 45555, 11, 286003, 49521, 11),
    (64, 413988, 393412, 418277, 20513, 417060, 41314, 49362),
    (265267, 131366, 139462, 139750, 404498, 434512, 151910, 16579),
    (82224, 264213, 65570, 24850, 307824, 422096, 99091, 241862),
    (467233, 110752, 37042, 429331, 156262, 82241, 65554, 281776),
    (348453, 107346, 65699, 164102, 266320, 28866, 28675, 429220),
    (160038, 107331, 151718, 49218, 139334, 90435, 131078, 392498),
    (446609, 181062, 430769, 16, 317460, 139462, 265488, 418032),
    (16514, 268341, 144038, 16387, 321541, 168262, 397717, 82145),
    (24707, 396304, 57664, 405509, 119313, 8193, 164230, 164070),
    (147590, 12, 2071, 167942, 246278, 53714, 12, 12),
    (278032, 414353, 12, 393396, 12, 184774, 90353, 426352),
    (367634, 205446, 70003, 155814, 408626, 277680, 8418, 209254),
    (365140, 277173, 205158, 91056, 404563, 273569, 159974, 12449),
    (188998, 82402, 41778, 86850, 73762, 45409, 86066, 36898),
    (12, 13, 95011, 12, 2231, 438992, 86051, 412723),
    (291028, 438420, 234278, 415761, 278544, 70339, 135206, 13),
    (155846, 155782, 13, 272388, 94210, 201414, 13, 272533),
    (273587, 168470, 86752, 410069, 81923, 12, 20627, 86113),
    (12466, 73810, 398164, 184774, 131078, 273488, 143494, 61459),
    (16547, 90179, 441651, 322356, 264564, 281665, 397748, 139270),
    (151718, 421956, 185158, 13, 280933, 27716, 237990, 2487),
    (302672, 192582, 310290, 115347, 363699, 420933, 277712, 53585),
    (277714, 28675, 2103, 180870, 13, 110706, 314561, 168262),
    (13, 453812, 11537, 280820, 287120, 20579, 2071, 379984),
    (462961, 119344, 437507, 147670, 176518, 147558, 49618, 416835),
    (266276, 430628, 201110, 106736, 33489, 384339, 16835, 76869),
    (226134, 420657, 78480, 159974, 221894, 437573, 188870, 421077),
    (295316, 301861, 115330, 273584, 37074, 13, 286035, 20643),
    (285810, 201254, 189062, 2103, 209094, 412113, 109716, 111314),
    (172422, 12290, 284789, 65650, 66194, 268741, 408709, 180934),
    (7, 41123, 297044, 176230, 17027, 107283, 127858, 2071),
    (7, 404530, 147606, 432209, 152198, 209670, 172902, 160278),
    (7, 284757, 221910, 61970, 268340, 131158, 94898, 82579),
    (7, 367824, 155734, 258566, 264229, 429300, 53923, 225926),
    (7, 426740, 408016, 289044, 3063, 114739, 217766, 326930),
    (7, 442484, 317892, 58274, 45617, 392304, 2103, 152406),
    (7, 172774, 24579, 286000, 201254, 314465, 2167, 272436),
    (7, 147558, 176726, 123571, 2135, 31844, 28961, 405589),
    (7, 36898, 399664, 172710, 276628, 32771, 37154, 155718),
    (7, 401412, 330021, 99139, 268421, 280725, 193014, 425075),
    (7, 297941, 246678, 143510, 290067, 450800, 2199, 305940),
    (7, 53619, 338325, 196918, 2167, 57571, 78019, 359317),
    (7, 143718, 45170, 2231, 7, 196838, 445456, 284756),
    (7, 428305, 217190, 250294, 7, 396338, 35845, 2167),
    (7, 407665, 415889, 292980, 7, 447344, 74354, 7),
    (7, 399458, 292996, 434517, 7, 45923, 49763, 7),
    (7, 101745, 7, 225606, 7, 156518, 201318, 7),
    (7, 306448, 7, 2679, 7, 32802, 421044, 7),
    (7, 7, 7, 424465, 7, 2167, 126117, 7),
    (7, 7, 7, 7, 7, 90706, 2135, 7),
    (7, 7, 7, 7, 7, 188998, 147574, 7),
    (7, 7, 7, 7, 7, 62131, 33041, 7),
    (7, 7, 7, 7, 7, 217766, 102658, 7),
    (7, 7, 7, 7, 7, 2071, 180486, 7),
    (7, 7, 7, 7, 7, 15381, 359536, 7),
    (7, 7, 7, 7, 7, 234326, 7, 7),
    (7, 7, 7, 7, 7, 322931, 7, 7),
    (7, 7, 7, 7, 7, 441701, 7, 7),
    (7, 7, 7, 7, 7, 213750, 7, 7),
    (7, 7, 7, 7, 7, 288821, 7, 7),
    (7, 7, 7, 7, 7, 237750, 7, 7),
    (7, 7, 7, 7, 7, 313428, 7, 7),
    (7, 7, 7, 7, 7, 250806, 7, 7),
    (7, 7, 7, 7, 7, 375796, 7, 7),
    (7, 7, 7, 7, 7, 343013, 7, 7),
    (7, 7, 7, 7, 7, 442672, 7, 7),
    (7, 7, 7, 7, 7, 119073, 7, 7),
    (7, 7, 7, 7, 7, 172326, 7, 7),
    (7, 7, 7, 7, 7, 180374, 7, 7),
    (7, 7, 7, 7, 7, 330325, 7, 7),
    (7, 7, 7, 7, 7, 335315, 7, 7),
    (7, 7, 7, 7, 7, 433362, 7, 7),
    (7, 7, 7, 7, 7, 2871, 7, 7),
    (7, 7, 7, 7, 7, 343475, 7, 7),
    (385973, 2199, 33091, 7, 70049, 41490, 462228, 217782),
    (246694, 2487, 7, 7, 33186, 258566, 69809, 254230),
    (306608, 77859, 7, 7, 82225, 2391, 176294, 49633),
    (127664, 2263, 7, 7, 164134, 314898, 7, 7),
    (471713, 306321, 7, 7, 160342, 325813, 7, 7),
    (58018, 380016, 7, 7, 295088, 425364, 7, 7),
    (209574, 7, 7, 7, 213158, 2263, 7, 7),
    (339090, 7, 7, 7, 7, 2967, 7, 7),
    (40960, 7, 7, 7, 7, 7, 7, 7),
    (277875, 326197, 2231, 7, 338229, 40993, 293204, 143510),
    (213718, 32081, 159990, 7, 301268, 7, 7, 301236),
    (7, 424113, 115667, 7, 288965, 7, 7, 7),
    (7, 305317, 164806, 7, 82162, 7, 7, 7),
    (7, 7, 7, 7, 205030, 7, 7, 7),
    (7, 2295, 404564, 309396, 110723, 2295, 331123, 309556),
    (7, 7, 93253, 330100, 314578, 426256, 62161, 7),
    (7, 7, 301268, 2647, 291696, 49409, 221894, 7),
    (7, 7, 7, 7, 62306, 123138, 298032, 7),
    (7, 7, 7, 7, 226150, 160006, 7, 7),
    (7, 7, 7, 7, 7, 65538, 7, 7),
    (319024, 2455, 294064, 310512, 412786, 164822, 213654, 147862),
    (164118, 176918, 305429, 94610, 2999, 455088, 363252, 213974),
    (281843, 102611, 309492, 53635, 2391, 86435, 293605, 321748),
    (340212, 123344, 107280, 237958, 321812, 225702, 2231, 338388),
    (286949, 151750, 168710, 58275, 354565, 2775, 335152, 197622),
    (168166, 225734, 94514, 318577, 98433, 7, 2263, 123761),
    (409043, 185270, 229670, 209622, 297460, 7, 301300, 115555),
    (7, 2391, 7, 205718, 349008, 7, 305381, 234342),
    (7, 383445, 7, 334036, 111425, 7, 318704, 346388),
    (7, 318546, 7, 411953, 238406, 7, 7, 185078),
    (7, 159990, 7, 7, 254966, 7, 7, 2423),
    (7, 445009, 7, 7, 2807, 7, 7, 73763),
    (7, 375365, 7, 7, 2455, 7, 7, 2295),
    (7, 164118, 7, 7, 385936, 7, 7, 7),
    (7, 7, 7, 7, 115585, 7, 7, 7),
    (7, 7, 7, 7, 197510, 7, 7, 7),
    (7, 7, 7, 7, 342260, 7, 7, 7),
    (7, 7, 7, 7, 297189, 7, 7, 7),
    (7, 7, 7, 7, 2935, 7, 7, 7),
    (86050, 7, 254230, 229750, 119059, 338708, 78593, 70577),
    (331376, 7, 53987, 342420, 168198, 78481, 242006, 250790),
    (184854, 7, 400437, 2391, 102530, 410244, 2327, 7),
    (332149, 7, 2391, 354740, 172374, 254598, 2359, 7),
    (176486, 7, 7, 54080, 188886, 433428, 69698, 7),
    (302387, 7, 7, 7, 7, 7, 412273, 7),
    (180566, 7, 7, 7, 7, 7, 7, 7),
    (7, 217430, 7, 127955, 338612, 98931, 7, 74033),
    (7, 2711, 7, 254918, 326309, 176742, 7, 172326),
    (7, 2359, 7, 7, 7, 366869, 7, 2679),
    (7, 310512, 7, 7, 7, 7, 7, 395600),
    (363795, 115376, 7, 404529, 314611, 372211, 185174, 7),
    (7, 66210, 7, 338979, 180598, 7, 7, 7),
    (7, 209574, 7, 189174, 7, 7, 7, 7),
    (7, 230294, 7, 2839, 7, 7, 7, 7),
    (7, 347536, 180790, 2519, 57379, 354612, 318004, 7),
    (7, 346997, 127011, 7, 7, 350613, 403856, 7),
    (7, 213398, 330100, 7, 7, 2423, 342404, 7),
    (7, 2423, 334325, 7, 7, 7, 375173, 7),
    (7, 7, 238006, 7, 7, 7, 246678, 7),
    (7, 7, 354740, 7, 7, 7, 2423, 7),
    (7, 7, 346533, 7, 7, 7, 7, 7),
    (7, 7, 193014, 7, 7, 7, 7, 7),
    (319989, 123315, 70096, 330896, 326068, 221590, 334357, 2455),
    (192998, 188838, 74179, 201270, 334245, 391669, 7, 94802),
    (327059, 2967, 213446, 7, 360944, 7, 7, 193094),
    (287156, 197622, 420369, 7, 192998, 7, 7, 2647),
    (344485, 7, 363012, 7, 347092, 7, 7, 121877),
    (197030, 7, 424881, 7, 351173, 7, 7, 7),
    (311860, 7, 359333, 7, 364960, 7, 7, 7),
    (201254, 7, 7, 7, 7, 7, 7, 7),
    (319956, 7, 7, 7, 7, 7, 7, 7),
    (373189, 7, 7, 7, 7, 7, 7, 7),
    (205254, 7, 7, 7, 7, 7, 7, 7),
    (77859, 358901, 7, 351251, 2519, 7, 7, 188854),
    (7, 7, 7, 2551, 7, 7, 7, 420721),
    (7, 7, 7, 2615, 7, 7, 7, 7),
    (7, 7, 7, 425040, 7, 7, 7, 7),
    (396372, 221814, 111218, 213590, 7, 119698, 358836, 205270),
    (380242, 2583, 90723, 7, 7, 230278, 350629, 7),
    (217718, 7, 209510, 7, 7, 205302, 254934, 7),
    (455313, 7, 197142, 7, 7, 2487, 197206, 7),
    (221830, 7, 7, 7, 7, 102946, 2519, 7),
    (7, 127856, 379765, 7, 2583, 383509, 371189, 99121),
    (7, 111458, 7, 7, 2615, 7, 7, 238374),
    (7, 234342, 7, 7, 7, 7, 7, 362996),
    (7, 7, 7, 7, 7, 7, 7, 94691),
    (110690, 246358, 259062, 222070, 2647, 2615, 205334, 221750),
    (7, 7, 2615, 98928, 412819, 432753, 209462, 2615),
    (7, 7, 355536, 217702, 367380, 379492, 78594, 2583),
    (7, 7, 371857, 367284, 371461, 387733, 363601, 359568),
    (7, 7, 7, 2711, 2679, 7, 7, 375937),
    (7, 7, 7, 392401, 7, 7, 7, 7),
    (348948, 2679, 371316, 7, 217782, 375952, 2647, 230006),
    (230150, 2775, 2647, 7, 355635, 7, 7, 371348),
    (7, 242390, 7, 7, 2711, 7, 7, 7),
    (127043, 7, 2711, 119795, 7, 7, 250806, 7),
    (323685, 7, 7, 234470, 7, 7, 2871, 7),
    (234294, 7, 7, 7, 7, 7, 7, 7),
    (238326, 258870, 7, 379604, 7, 2743, 7, 376051),
    (347632, 7, 7, 7, 7, 7, 7, 2743),
    (353140, 2807, 380144, 246550, 2871, 246774, 408209, 2775),
    (340837, 2839, 7, 2807, 127761, 2807, 387716, 2807),
    (242534, 7, 7, 115504, 230150, 123697, 234230, 246550),
    (7, 7, 7, 242470, 234294, 242470, 7, 2871),
    (7, 7, 7, 7, 2775, 7, 7, 2903),
    (7, 7, 7, 7, 242422, 7, 7, 7),
    (7, 392497, 383700, 2903, 250806, 7, 226102, 7),
    (7, 7, 2743, 7, 7, 7, 2743, 7),
    (7, 7, 127856, 7, 7, 7, 383700, 7),
    (7, 7, 242534, 7, 7, 7, 383685, 7),
    (7, 7, 2807, 7, 7, 7, 7, 7),
    (7, 7, 7, 388052, 7, 2903, 7, 7),
    (7, 7, 7, 2935, 7, 2935, 7, 7),
    (368708, 7, 7, 2967, 2903, 7, 7, 7),
    (7, 7, 7, 7, 125840, 7, 7, 7),
    (385940, 2903, 2839, 2999, 7, 7, 2839, 258966),
    (357253, 7, 2871, 7, 7, 7, 3063, 7),
    (250758, 7, 2903, 7, 7, 7, 7, 7),
    (102496, 7, 7, 7, 7, 7, 7, 7),
    (102499, 7, 7, 7, 7, 7, 7, 7),
    (7, 7, 250806, 7, 7, 7, 7, 2999),
    (102466, 2999, 7, 7, 7, 2999, 7, 7),
    (381028, 7, 7, 7, 7, 7, 7, 7),
    (7, 254934, 7, 7, 7, 3031, 2903, 7),
    (7, 7, 7, 7, 7, 7, 392117, 7),
    (7, 7, 7, 7, 7, 7, 2935, 7),
    (254934, 3063, 392305, 3063, 7, 7, 2967, 7),
    (7, 7, 2967, 7, 7, 7, 388053, 7),
    (7, 7, 7, 7, 7, 7, 259062, 7),
    (259062, 7, 3031, 7, 259030, 7, 7, 3031),
    (7, 7, 3063, 7, 7, 7, 7, 3063),
)
SEGMENTS = (83, 9, 5, 6, 19, 7, 4, 4, 8, 11, 4, 5, 4, 6, 3, 3, 2, 6, 5, 2, 2, 5, 1, 2, 3, 3, 0, 0, 2, 0, 0, 0, 0)
BLOCKS = (
    (803072, 407081, 298570, 232800, 139664, 295597, 47690, 758240),
    (297348, 108580, 198080, 37196, 1023284, 331874, 153827, 920811),
    (460134, 185346, 494133, 317890, 33261, 170236, 175317, 726225),
    (617635, 839516, 421861, 518335, 600963, 903001, 2615, 1028706),
    (583559, 1043950, 996584, 268722, 194007, 734123, 835437, 1009098),
    (1029743, 751878, 856441, 587516, 826187, 539231, 1028944, 880208),
    (1013076, 816651, 816851, 1003285, 916246, 56990, 315326, 657064),
    (748277, 610551, 679452, 545657, 640085, 806376, 815380, 325048),
)
OWN = ((0, 5, 10, 2, 3, 11, 9, 5), (1, 0, 0, 1, 1, 0, 2, 1), (2, 1, 1, 26, 4, 1, 6, 3), (3, 15, 23, 29, 13, 17, 24, 15))
PARTNERS = ((0, 2, 10, 5, 3, 5, 9, 11), (1, 1, 0, 0, 1, 1, 2, 0), (2, 26, 1, 1, 4, 3, 6, 1), (3, 29, 23, 15, 13, 15, 24, 17))
TRANSIT = 20
TI = 512

ROWS, COLS, RANK, HALF = 2048, 1024, 64, 1024
OTHER, COL_SLOT, TRANSIT_SLOT = 32, 64, 96
SLOTS = TRANSIT_SLOT + TRANSIT
NI = len(ITEMS)


def split(x):
    high = x.astype(BF16)
    return high, (x - high.astype(F32)).astype(BF16)


def kernel(
    trailing, factors, vectors, inverse, slots, acc,
    buf, right, wide, block_core, part, by_row, total, cores, known, table,
    local_sem, recv_sem, send_sem, own_send, row_send, row_recv, col_send, col_recv,
):
    r, c = lax.axis_index("row"), lax.axis_index("col")
    z, x, y, k = r // 2, (r % 2) * 2 + (c // 2) % 2, c // 4, c % 2
    flip = x // 2
    sx, sy = 1 - 2 * flip, 1 - 2 * k
    xc = x + flip * (3 - 2 * x)
    delta = (sy * (y - z) + 4) % 4
    kind = xc * 4 + delta
    diagonal = jnp.where(kind == 0, 1, 0)
    q = c // 2

    def device(x, y, z, k):
        return (z * 2 + x // 2, y * 4 + (x % 2) * 2 + k)

    partner = (r, q * 2 + 1 - k)
    row_peers = [((r + i) % 8, c) for i in range(1, 8)]
    col_peers = [(r, (c + 2 * i) % 16) for i in range(1, 8)]
    outer = device(3 - x, y, z, k)

    start_acc = pltpu.make_async_copy(trailing, acc, local_sem.at[4])
    start_acc.start()
    bits = [kind % 2 == 1, (kind // 2) % 2 == 1, kind // 4 == 1]

    def pick(row):
        pairs = [jnp.where(bits[0], I32(row[2 * a + 1]), I32(row[2 * a])) for a in range(4)]
        pairs = [jnp.where(bits[1], pairs[2 * a + 1], pairs[2 * a]) for a in range(2)]
        return jnp.where(bits[2], pairs[1], pairs[0])

    own = []
    for j in range(2):
        here = jnp.where(k == 0, pick(OWN[j]), pick(OWN[2 + j]))
        there = jnp.where(k == 0, pick(PARTNERS[j]), pick(PARTNERS[2 + j]))
        for h in range(2):
            src = factors.at[pl.ds(j * RANK, RANK), pl.ds(h * HALF, HALF)]
            other = jnp.where(k == h, 0, 1)
            slot = here + OTHER * other
            own.append((src, there + OTHER * (1 - other)))
            pltpu.make_async_copy(src, buf.at[slot], recv_sem.at[slot]).start()

    barrier = pltpu.get_barrier_semaphore()
    greeted = row_peers + col_peers + [outer, partner]
    for peer in greeted:
        pl.semaphore_signal(barrier, inc=1, device_id=peer, device_id_type=MESH)

    for i, row in enumerate(ITEMS):
        table[i] = pick(row)

    nt = (((1,), (1,)), ((), ()))
    blank = jnp.zeros((RANK, RANK * 8), F32)
    first = lax.dot_general(
        vectors[0], jnp.concatenate([inverse[0], blank], axis=0), nt,
        precision=lax.Precision.HIGHEST, preferred_element_type=F32,
    )
    second = lax.dot_general(
        vectors[1], jnp.concatenate([blank, inverse[1]], axis=0), nt,
        precision=lax.Precision.HIGHEST, preferred_element_type=F32,
    )
    blank = jnp.zeros((RANK, 2 * RANK), F32)
    part[...] = lax.dot_general(
        first, jnp.concatenate([first, blank], axis=0), nt,
        precision=lax.Precision.HIGHEST, preferred_element_type=F32,
    ) + lax.dot_general(
        second, jnp.concatenate([blank, second], axis=0), nt,
        precision=lax.Precision.HIGHEST, preferred_element_type=F32,
    )
    block_core[...] = jnp.zeros_like(block_core)

    pl.semaphore_wait(barrier, len(greeted))

    own_copies = []
    for i, (src, slot) in enumerate(own):
        copy = pltpu.make_async_remote_copy(
            src_ref=src, dst_ref=buf.at[slot], send_sem=own_send.at[i], recv_sem=recv_sem.at[slot],
            device_id=partner, device_id_type=MESH,
        )
        copy.start()
        own_copies.append(copy)

    def arrived(slot):
        pltpu.make_async_copy(buf.at[slot], buf.at[slot], recv_sem.at[slot]).wait()

    def panel_at(code):
        block = 2 * ((sy * (code % 4) + z + 4) % 4) + (code // 4 + flip) % 2
        return 4 * block + code // 8

    def send_of(i, word):
        way = word % 16
        src, dst = (word // 32) % 128, (word // 4096) % 128
        axis, turn = way // 2, 1 - 2 * (way % 2)
        dx = jnp.where(axis == 0, sx * turn, 0)
        dy = jnp.where(axis == 1, sy * turn, 0)
        dz = jnp.where(axis == 2, sy * turn, 0)
        dk = jnp.where(axis == 3, 1, 0)
        target = device((x + dx + 4) % 4, (y + dy + 4) % 4, (z + dz + 4) % 4, (k + dk) % 2)
        return src, pltpu.make_async_remote_copy(
            src_ref=buf.at[src], dst_ref=buf.at[dst], send_sem=send_sem.at[i],
            recv_sem=recv_sem.at[dst], device_id=target, device_id_type=MESH,
        )

    def pass_on(i, word):
        src, copy = send_of(i, word)

        @pl.when((word // 16) % 2 == 1)
        def _():
            arrived(src)

        @pl.when(word % 16 < 7)
        def _():
            copy.start()

    def moves(i, _):
        pass_on(i, table[i])
        return 0

    def sent(i, _):
        @pl.when(table[i] % 16 < 7)
        def _():
            pltpu.make_async_copy(buf.at[0], buf.at[0], send_sem.at[i]).wait()

        return 0

    def prepare(block):
        codes = pick(BLOCKS[block])
        for a in range(4):
            place = 4 * block + a
            arrived(OTHER + place)
            panel = panel_at((codes // (1 << (5 * a))) % 32)
            high, low = split(buf[jnp.where(diagonal == 1, place, COL_SLOT + place)])
            wide[pl.ds(a * RANK, RANK)] = high
            wide[pl.ds(256 + a * RANK, RANK)] = high
            wide[pl.ds(512 + a * RANK, RANK)] = low
            slot = slots[panel]
            pair = known[(slot // 2) % 2 * 8 + slot // 4]
            lane = lax.broadcasted_iota(I32, (RANK, 2 * RANK), 1) // RANK
            same = jnp.where(slot % 2 == a % 2, F32(1), F32(0))
            moved = pair * same + pltpu.roll(pair, RANK, axis=1) * (F32(1) - same)
            block_core[pl.ds(a * RANK, RANK), pl.ds((a // 2) * 128, 128)] = jnp.where(
                lane == a % 2, moved, F32(0)
            )
        high, low = split(block_core[...])
        scaled = jnp.dot(
            jnp.concatenate([high, low, high], axis=1), wide[...], preferred_element_type=F32
        )
        high, low = split(scaled)
        right[0:256] = high
        right[256:512] = high
        right[512:768] = low

    def tile_rows(j):
        h = k if j * TI < HALF else 1 - k
        return pl.ds(pl.multiple_of(h * HALF + (j * TI) % HALF, TI), TI)

    def tile(block, j):
        if j == 0:
            prepare(block)
        base = 4 * block + (0 if j * TI < HALF else OTHER)
        left = buf[base : base + 4, :, (j * TI) % HALF : (j * TI) % HALF + TI]
        high, low = split(left.reshape(256, TI))
        rows = tile_rows(j)
        acc[rows] = acc[rows] - lax.dot_general(
            jnp.concatenate([high, low, high], axis=0), right[...], (((0,), (0,)), ((), ())),
            preferred_element_type=F32,
        )

    mine = k * 8 + q
    row_copies = [
        pltpu.make_async_remote_copy(
            src_ref=part, dst_ref=by_row.at[6 - i], send_sem=row_send.at[i],
            recv_sem=row_recv.at[6 - i], device_id=peer, device_id_type=MESH,
        )
        for i, peer in enumerate(row_peers)
    ]
    keep = pltpu.make_async_copy(total, cores.at[mine], local_sem.at[5])
    col_copies = [
        pltpu.make_async_remote_copy(
            src_ref=total, dst_ref=cores.at[mine], send_sem=col_send.at[i],
            recv_sem=col_recv.at[i], device_id=peer, device_id_type=MESH,
        )
        for i, peer in enumerate(col_peers)
    ]
    half = cores.at[pl.ds(k * 8, 8)]
    exchange = pltpu.make_async_remote_copy(
        src_ref=half, dst_ref=half, send_sem=col_send.at[7], recv_sem=col_recv.at[7],
        device_id=partner, device_id_type=MESH,
    )
    settle = pltpu.make_async_copy(cores, known, local_sem.at[6])

    def give_share():
        for copy in row_copies:
            copy.start()

    def add_shares():
        for i in range(7):
            pltpu.make_async_copy(part, by_row.at[i], row_recv.at[i]).wait()
        summed = part[...]
        for i in range(7):
            summed = summed + by_row[i]
        total[...] = summed

    def give_total():
        keep.start()
        for copy in col_copies:
            copy.start()

    def give_half():
        keep.wait()
        for i in range(7):
            sender = k * 8 + (q + 7 - i) % 8
            pltpu.make_async_copy(total, cores.at[sender], col_recv.at[i]).wait()
        exchange.start()

    def take_half():
        exchange.wait_recv()
        settle.start()
        settle.wait()
        start_acc.wait()

    def opening(i, _):
        word = table[i]

        @pl.when(word % 16 < 8)
        def _():
            pass_on(i, word)

        for phase, action in enumerate((give_share, add_shares, give_total, give_half, take_half)):
            pl.when(word % 16 == 9 + phase)(action)
        return 0

    lax.fori_loop(0, SEGMENTS[0], opening, 0)
    tiles = ROWS // TI
    done = SEGMENTS[0]
    end = checked = 0
    for t, length in enumerate(SEGMENTS):
        end += length
        if end > done:
            lax.fori_loop(done, end, moves, 0)
            done = end
        if t in (4 * tiles, 7 * tiles):
            early = sum(SEGMENTS[: t - tiles])
            lax.fori_loop(checked, early, sent, 0)
            checked = early
        if t < 8 * tiles:
            tile(t // tiles, t % tiles)

    for copy in own_copies + row_copies + col_copies + [exchange]:
        copy.wait_send()

    lax.fori_loop(checked, NI, sent, 0)


def body(trailing, panel_factors, vectors_t, inverse_lower_factors, slot_of_panel):
    hbm = pl.BlockSpec(memory_space=pl.ANY)
    vmem = pl.BlockSpec(memory_space=pltpu.VMEM)
    dma = pltpu.SemaphoreType.DMA
    return pl.pallas_call(
        kernel,
        out_shape=pltpu.VMEM((ROWS, COLS), F32),
        in_specs=[hbm, hbm, vmem, vmem, pl.BlockSpec(memory_space=pltpu.SMEM)],
        out_specs=vmem,
        scratch_shapes=[
            pltpu.VMEM((SLOTS, RANK, HALF), F32),
            pltpu.VMEM((768, COLS), BF16),
            pltpu.VMEM((768, COLS), BF16),
            pltpu.VMEM((256, 256), F32),
            pltpu.VMEM((RANK, 2 * RANK), F32),
            pltpu.VMEM((7, RANK, 2 * RANK), F32),
            pltpu.VMEM((RANK, 2 * RANK), F32),
            pltpu.VMEM((16, RANK, 2 * RANK), F32),
            pltpu.VMEM((16, RANK, 2 * RANK), F32),
            pltpu.SMEM((NI,), I32),
            dma((7,)), dma((SLOTS,)), dma((NI,)), dma((4,)), dma((7,)), dma((7,)), dma((8,)), dma((8,)),
        ],
        compiler_params=pltpu.CompilerParams(
            collective_id=0, has_side_effects=True, vmem_limit_bytes=55 * 2**20
        ),
        name="update",
    )(trailing, panel_factors, vectors_t, inverse_lower_factors, slot_of_panel)


def solution(mesh):
    return jax.shard_map(
        body,
        mesh=mesh,
        in_specs=(
            P("row", "col"),
            P("col", "row"),
            P("col", None, None),
            P("col", "row", None),
            P(),
        ),
        out_specs=P("row", "col"),
        check_vma=False,
    )
```

```python
import jax
import jax.numpy as jnp
from jax import lax
from jax.experimental import pallas as pl
from jax.experimental.pallas import tpu as pltpu
from jax.sharding import PartitionSpec as P

MESH = pl.DeviceIdType.MESH
F32, BF16, I32 = jnp.float32, jnp.bfloat16, jnp.int32

ITEMS = (
    (9, 9, 9, 9, 9, 9, 9, 9),
    (8240, 24754, 16, 24656, 16497, 430096, 20561, 65585),
    (458769, 397476, 33106, 426049, 24674, 45426, 41267, 393397),
    (36866, 10, 10, 36914, 413748, 78179, 10, 10),
    (262181, 61488, 4144, 10, 262288, 10, 106705, 430192),
    (10, 74259, 20482, 86051, 10, 107057, 90179, 65634),
    (3, 11, 11, 394069, 33203, 11, 11, 49251),
    (266325, 12304, 58098, 11, 413733, 401956, 45250, 397845),
    (11, 8496, 28882, 45587, 11, 286003, 49521, 11),
    (64, 413988, 393412, 418309, 20513, 417060, 41314, 49362),
    (265267, 131366, 139462, 139782, 404498, 434512, 151910, 16579),
    (82224, 264213, 69666, 24850, 307824, 422096, 99091, 237766),
    (467233, 106656, 45234, 429331, 156262, 82241, 69650, 281776),
    (348453, 99154, 61603, 164102, 266320, 28866, 28675, 429220),
    (160038, 107331, 151718, 49218, 139334, 90435, 131078, 392498),
    (446609, 168774, 430769, 16, 317460, 139462, 265488, 418064),
    (16514, 268341, 144038, 16387, 325637, 168262, 397717, 82177),
    (24707, 396304, 57664, 405509, 119313, 8193, 164230, 164102),
    (147590, 12, 2071, 167942, 250374, 53746, 12, 12),
    (278032, 414353, 12, 393396, 12, 184806, 90353, 426352),
    (367634, 205446, 74099, 155814, 408626, 277680, 8418, 209254),
    (365140, 277173, 209254, 78768, 404563, 273569, 159974, 12449),
    (188998, 82434, 41810, 86850, 73762, 45409, 90162, 36898),
    (12, 13, 99139, 12, 2231, 438992, 86051, 412723),
    (291028, 438420, 238406, 415761, 278544, 74435, 135206, 13),
    (155846, 155782, 13, 272388, 94210, 205510, 13, 272533),
    (273587, 176630, 90848, 410069, 86019, 12, 20627, 86113),
    (12466, 77906, 398100, 184774, 131078, 273488, 143494, 65555),
    (16547, 90179, 441651, 322356, 264564, 281665, 397748, 139270),
    (151718, 421956, 185094, 13, 280933, 27716, 246182, 2487),
    (302672, 196678, 314386, 115347, 363699, 420933, 277712, 53585),
    (277714, 28675, 2103, 180870, 13, 110706, 314561, 168262),
    (13, 453812, 11537, 280820, 287120, 20579, 2071, 379984),
    (462961, 420657, 437507, 147670, 176518, 147558, 49618, 416835),
    (266276, 301861, 197014, 102640, 33489, 376147, 16835, 72773),
    (226134, 123472, 74384, 159974, 221894, 437573, 188870, 421077),
    (295316, 430660, 111234, 273584, 37074, 13, 286035, 20643),
    (285810, 193094, 189062, 2103, 209094, 412145, 113812, 107122),
    (172422, 12290, 284789, 65650, 66194, 268773, 408709, 180838),
    (7, 41123, 297044, 176230, 17027, 115475, 123762, 2071),
    (7, 404530, 147606, 432209, 152198, 213766, 172902, 160310),
    (7, 284757, 221910, 62002, 268340, 131158, 107218, 86707),
    (7, 367824, 155734, 258598, 264229, 429300, 53955, 225958),
    (7, 426772, 408016, 289044, 3063, 118835, 221894, 326930),
    (7, 442484, 317892, 58274, 45649, 392304, 2103, 152374),
    (7, 172806, 24579, 286000, 205382, 314465, 2167, 272436),
    (7, 147558, 176758, 123571, 2135, 31844, 28961, 405589),
    (7, 36898, 399664, 172710, 276628, 32771, 37154, 155718),
    (7, 401412, 334117, 103235, 268421, 280725, 197142, 425075),
    (7, 297941, 246678, 143510, 290067, 450800, 2199, 305940),
    (7, 53619, 338325, 192886, 2167, 57571, 78019, 359317),
    (7, 143718, 49266, 2231, 7, 200934, 445456, 284756),
    (7, 428305, 217190, 250294, 7, 396338, 31749, 2167),
    (7, 407665, 415889, 292980, 7, 447312, 62034, 7),
    (7, 399458, 292996, 434517, 7, 45891, 49731, 7),
    (7, 93553, 7, 229702, 7, 156486, 193094, 7),
    (7, 306448, 7, 424497, 7, 32802, 421044, 7),
    (7, 7, 7, 2679, 7, 2167, 130213, 7),
    (7, 7, 7, 7, 7, 82514, 2135, 7),
    (7, 7, 7, 7, 7, 188998, 147574, 7),
    (7, 7, 7, 7, 7, 62131, 33041, 7),
    (7, 7, 7, 7, 7, 221862, 94466, 7),
    (7, 7, 7, 7, 7, 2071, 180486, 7),
    (7, 7, 7, 7, 7, 15381, 359536, 7),
    (7, 7, 7, 7, 7, 226166, 7, 7),
    (7, 7, 7, 7, 7, 322931, 7, 7),
    (7, 7, 7, 7, 7, 441701, 7, 7),
    (7, 7, 7, 7, 7, 217846, 7, 7),
    (7, 7, 7, 7, 7, 288821, 7, 7),
    (7, 7, 7, 7, 7, 233654, 7, 7),
    (7, 7, 7, 7, 7, 313428, 7, 7),
    (7, 7, 7, 7, 7, 250838, 7, 7),
    (7, 7, 7, 7, 7, 371700, 7, 7),
    (7, 7, 7, 7, 7, 338917, 7, 7),
    (7, 7, 7, 7, 7, 442672, 7, 7),
    (7, 7, 7, 7, 7, 119073, 7, 7),
    (7, 7, 7, 7, 7, 172326, 7, 7),
    (7, 7, 7, 7, 7, 180374, 7, 7),
    (7, 7, 7, 7, 7, 334421, 7, 7),
    (7, 7, 7, 7, 7, 339411, 7, 7),
    (7, 7, 7, 7, 7, 433362, 7, 7),
    (7, 7, 7, 7, 7, 2871, 7, 7),
    (7, 7, 7, 7, 7, 343475, 7, 7),
    (385973, 2199, 33091, 7, 70049, 41490, 462228, 217814),
    (246694, 2487, 2231, 7, 33186, 254470, 65713, 250102),
    (306608, 77859, 7, 7, 82225, 2391, 176294, 37377),
    (127664, 2263, 7, 7, 164134, 314898, 7, 7),
    (471713, 306321, 7, 7, 160310, 329909, 7, 7),
    (58018, 380016, 7, 7, 295088, 425364, 7, 7),
    (209574, 7, 7, 7, 213158, 2263, 7, 7),
    (334994, 7, 7, 7, 7, 2967, 7, 7),
    (40960, 7, 7, 7, 7, 7, 7, 7),
    (277875, 32081, 159990, 7, 338229, 40993, 293204, 143510),
    (213718, 424113, 115667, 7, 301268, 7, 7, 301236),
    (7, 305317, 164806, 7, 288965, 7, 7, 7),
    (7, 326229, 404564, 7, 82162, 7, 7, 7),
    (7, 7, 97349, 7, 200934, 7, 7, 7),
    (7, 7, 301268, 309396, 110723, 2295, 331123, 309556),
    (7, 7, 7, 334228, 314578, 426256, 62097, 7),
    (7, 7, 7, 7, 291664, 49409, 213638, 7),
    (7, 7, 7, 7, 58178, 123138, 298032, 7),
    (7, 7, 7, 7, 226118, 164102, 7, 7),
    (7, 7, 7, 7, 7, 69634, 7, 7),
    (319024, 2295, 294064, 2647, 412786, 160694, 217782, 147862),
    (164118, 2455, 305429, 310512, 2935, 455088, 363252, 214006),
    (281843, 180950, 309492, 94514, 2391, 86435, 297701, 321748),
    (340212, 102611, 115504, 53539, 321812, 237990, 2231, 342484),
    (286949, 119248, 168742, 237862, 354565, 2775, 326960, 197590),
    (168166, 151750, 90418, 209654, 98433, 7, 2263, 127857),
    (409043, 221638, 233766, 58275, 293364, 7, 301300, 107363),
    (7, 185270, 7, 318577, 349072, 7, 305381, 234342),
    (7, 318546, 7, 201590, 111489, 7, 318704, 350452),
    (7, 2391, 7, 329940, 246662, 7, 74497, 185174),
    (7, 383445, 7, 338228, 254966, 7, 7, 2423),
    (7, 159990, 7, 7, 2807, 7, 7, 77859),
    (7, 444977, 7, 7, 2455, 7, 7, 2327),
    (7, 375333, 7, 7, 385968, 7, 7, 7),
    (7, 164118, 7, 7, 115617, 7, 7, 7),
    (7, 7, 7, 7, 197542, 7, 7, 7),
    (7, 7, 7, 7, 346356, 7, 7, 7),
    (7, 7, 7, 7, 297189, 7, 7, 7),
    (7, 7, 7, 7, 2903, 7, 7, 7),
    (86050, 7, 254230, 412017, 119059, 334612, 242006, 62385),
    (331376, 7, 53987, 221590, 168198, 433428, 2327, 254886),
    (184854, 7, 400437, 2391, 102530, 78481, 2359, 7),
    (336245, 7, 2391, 354740, 172374, 410244, 73794, 7),
    (176486, 7, 7, 54080, 188886, 258694, 412241, 7),
    (310579, 7, 7, 7, 7, 7, 7, 7),
    (180566, 7, 7, 7, 7, 7, 7, 7),
    (7, 2359, 7, 127987, 326324, 103027, 185238, 74033),
    (7, 217430, 7, 254950, 322213, 176742, 7, 172326),
    (7, 2711, 7, 7, 7, 366869, 7, 2711),
    (7, 310512, 7, 7, 7, 380403, 7, 395600),
    (363795, 115376, 7, 404529, 314611, 7, 7, 7),
    (7, 70306, 7, 343075, 180598, 7, 7, 7),
    (7, 209574, 7, 189142, 7, 7, 7, 7),
    (7, 230294, 7, 7, 7, 7, 7, 7),
    (7, 347536, 180758, 2839, 57379, 354612, 317940, 7),
    (7, 346997, 127011, 2519, 7, 2423, 403856, 7),
    (7, 2423, 326004, 7, 7, 354709, 342404, 7),
    (7, 213398, 326133, 7, 7, 7, 375173, 7),
    (7, 7, 229814, 7, 7, 7, 238422, 7),
    (7, 7, 7, 7, 7, 7, 2423, 7),
    (319989, 123315, 358836, 334992, 330164, 209302, 338485, 2455),
    (192998, 188838, 346533, 205302, 334245, 391637, 7, 113685),
    (331155, 7, 193014, 7, 365040, 7, 7, 94706),
    (287156, 7, 7, 7, 192998, 7, 7, 188902),
    (344485, 7, 7, 7, 351188, 7, 7, 2551),
    (197030, 7, 7, 7, 351173, 7, 7, 7),
    (299572, 7, 7, 7, 360864, 7, 7, 7),
    (201254, 7, 7, 7, 7, 7, 7, 7),
    (319956, 7, 7, 7, 7, 7, 7, 7),
    (373189, 7, 7, 7, 7, 7, 7, 7),
    (205254, 7, 7, 7, 7, 7, 7, 7),
    (77859, 2967, 61904, 351251, 2519, 119698, 7, 192950),
    (7, 201718, 70083, 2551, 7, 230278, 7, 420721),
    (7, 7, 213446, 2583, 7, 7, 7, 7),
    (7, 7, 420401, 7, 7, 7, 7, 7),
    (7, 7, 354852, 7, 7, 7, 7, 7),
    (7, 7, 424881, 7, 7, 7, 7, 7),
    (7, 7, 355237, 7, 7, 7, 7, 7),
    (396372, 358933, 7, 425040, 7, 192982, 358836, 205270),
    (380242, 225910, 7, 213590, 7, 7, 354725, 7),
    (217718, 2551, 7, 7, 7, 7, 254934, 7),
    (455313, 7, 7, 7, 7, 7, 201334, 7),
    (221830, 7, 7, 7, 7, 7, 2519, 7),
    (7, 7, 7, 7, 7, 7, 205302, 7),
    (7, 7, 7, 7, 7, 7, 367125, 7),
    (7, 7, 7, 7, 2583, 102946, 7, 99057),
    (7, 7, 7, 7, 2615, 2487, 7, 242406),
    (7, 7, 7, 7, 2647, 383509, 7, 363028),
    (110690, 242230, 115282, 98928, 343347, 2615, 209462, 94723),
    (7, 127856, 94787, 217702, 359220, 432753, 82690, 221782),
    (7, 111458, 205382, 371380, 375589, 383588, 367697, 2615),
    (7, 234342, 201270, 226198, 2679, 387733, 7, 2647),
    (7, 7, 375669, 2711, 7, 7, 7, 7),
    (348948, 2807, 347344, 7, 412819, 371856, 2679, 7),
    (230150, 2679, 259062, 7, 217782, 7, 250806, 7),
    (7, 7, 7, 7, 2711, 7, 7, 7),
    (122947, 246518, 2583, 388305, 7, 7, 2871, 230038),
    (327781, 7, 371284, 119763, 7, 7, 7, 379572),
    (234294, 7, 363665, 234438, 7, 7, 7, 2679),
    (238326, 7, 2679, 7, 7, 2743, 7, 7),
    (347632, 7, 7, 7, 7, 7, 7, 7),
    (357236, 254774, 2711, 379636, 2839, 2807, 387732, 376051),
    (340837, 2775, 371952, 2775, 127793, 246774, 383621, 371856),
    (242534, 2839, 7, 246550, 234278, 123697, 226102, 380033),
    (7, 7, 7, 115504, 230166, 242470, 408241, 2775),
    (7, 7, 7, 242470, 2775, 7, 383652, 7),
    (7, 7, 7, 7, 242550, 7, 7, 7),
    (7, 7, 7, 7, 238326, 7, 7, 7),
    (7, 392497, 7, 2903, 7, 2903, 2775, 246550),
    (7, 7, 7, 7, 7, 7, 234230, 2807),
    (7, 7, 383700, 388084, 7, 2935, 7, 2871),
    (368708, 7, 2743, 2935, 2967, 7, 7, 2903),
    (7, 7, 2807, 7, 125872, 7, 7, 7),
    (7, 7, 127856, 7, 7, 7, 7, 7),
    (7, 7, 242534, 7, 7, 7, 7, 7),
    (390036, 2903, 2839, 2967, 7, 7, 2839, 258966),
    (361349, 7, 2871, 2999, 7, 7, 2903, 7),
    (250758, 7, 7, 7, 7, 7, 3063, 7),
    (98400, 7, 7, 7, 7, 7, 7, 7),
    (102499, 7, 7, 7, 7, 7, 7, 7),
    (7, 7, 2903, 7, 7, 2999, 7, 2999),
    (7, 7, 7, 7, 7, 3031, 7, 7),
    (102466, 2999, 7, 7, 7, 7, 2935, 7),
    (381028, 259030, 7, 7, 7, 7, 7, 7),
    (254934, 7, 7, 3031, 7, 7, 388021, 7),
    (7, 7, 7, 7, 7, 7, 259062, 7),
    (7, 7, 7, 7, 7, 7, 2967, 7),
    (7, 3063, 250806, 7, 7, 7, 392149, 7),
    (7, 7, 392305, 7, 7, 7, 7, 7),
    (7, 7, 2967, 7, 7, 7, 7, 3031),
    (7, 7, 7, 7, 259030, 7, 7, 7),
    (259062, 7, 3031, 7, 7, 7, 7, 3063),
    (7, 7, 3063, 7, 7, 7, 7, 7),
)
SEGMENTS = (83, 9, 5, 6, 19, 7, 4, 4, 6, 11, 7, 7, 3, 5, 3, 3, 2, 7, 2, 1, 4, 5, 2, 2, 3, 2, 1, 1, 2, 0, 0, 0, 0)
BLOCKS = (
    (803072, 407081, 298570, 232800, 139664, 295597, 47690, 758240),
    (297348, 108580, 198080, 37196, 1023284, 331874, 153827, 560363),
    (460134, 185346, 494133, 482274, 33261, 170236, 175317, 726236),
    (617635, 479068, 421861, 452777, 600963, 585561, 887351, 832098),
    (583559, 1032057, 456967, 268879, 179127, 734123, 517536, 899423),
    (1029743, 994566, 856441, 968444, 826187, 539231, 1042956, 707102),
    (1013076, 816662, 809597, 839445, 93912, 755358, 316350, 682024),
    (748277, 610551, 679452, 672638, 640702, 802408, 815379, 959928),
)
OWN = ((0, 5, 10, 2, 3, 11, 9, 5), (1, 0, 0, 1, 1, 0, 2, 1), (2, 1, 1, 26, 4, 1, 6, 3), (3, 16, 23, 29, 13, 17, 24, 16))
PARTNERS = ((0, 2, 10, 5, 3, 5, 9, 11), (1, 1, 0, 0, 1, 1, 2, 0), (2, 26, 1, 1, 4, 3, 6, 1), (3, 29, 23, 16, 13, 16, 24, 17))
TRANSIT = 20
TI = 512

ROWS, COLS, RANK, HALF = 2048, 1024, 64, 1024
OTHER, COL_SLOT, TRANSIT_SLOT = 32, 64, 96
SLOTS = TRANSIT_SLOT + TRANSIT
NI = len(ITEMS)


def split(x):
    high = x.astype(BF16)
    return high, (x - high.astype(F32)).astype(BF16)


def kernel(
    trailing, factors, vectors, inverse, slots, acc,
    buf, right, wide, block_core, part, by_row, total, cores, known, table,
    local_sem, recv_sem, send_sem, own_send, row_send, row_recv, col_send, col_recv,
):
    r, c = lax.axis_index("row"), lax.axis_index("col")
    z, x, y, k = r // 2, (r % 2) * 2 + (c // 2) % 2, c // 4, c % 2
    flip = x // 2
    sx, sy = 1 - 2 * flip, 1 - 2 * k
    xc = x + flip * (3 - 2 * x)
    delta = (sy * (y - z) + 4) % 4
    kind = xc * 4 + delta
    diagonal = jnp.where(kind == 0, 1, 0)
    q = c // 2

    def device(x, y, z, k):
        return (z * 2 + x // 2, y * 4 + (x % 2) * 2 + k)

    partner = (r, q * 2 + 1 - k)
    row_peers = [((r + i) % 8, c) for i in range(1, 8)]
    col_peers = [(r, (c + 2 * i) % 16) for i in range(1, 8)]
    outer = device(3 - x, y, z, k)

    start_acc = pltpu.make_async_copy(trailing, acc, local_sem.at[4])
    start_acc.start()
    bits = [kind % 2 == 1, (kind // 2) % 2 == 1, kind // 4 == 1]

    def pick(row):
        pairs = [jnp.where(bits[0], I32(row[2 * a + 1]), I32(row[2 * a])) for a in range(4)]
        pairs = [jnp.where(bits[1], pairs[2 * a + 1], pairs[2 * a]) for a in range(2)]
        return jnp.where(bits[2], pairs[1], pairs[0])

    own = []
    for j in range(2):
        here = jnp.where(k == 0, pick(OWN[j]), pick(OWN[2 + j]))
        there = jnp.where(k == 0, pick(PARTNERS[j]), pick(PARTNERS[2 + j]))
        for h in range(2):
            src = factors.at[pl.ds(j * RANK, RANK), pl.ds(h * HALF, HALF)]
            other = jnp.where(k == h, 0, 1)
            slot = here + OTHER * other
            own.append((src, there + OTHER * (1 - other)))
            pltpu.make_async_copy(src, buf.at[slot], recv_sem.at[slot]).start()

    barrier = pltpu.get_barrier_semaphore()
    greeted = row_peers + col_peers + [outer, partner]
    for peer in greeted:
        pl.semaphore_signal(barrier, inc=1, device_id=peer, device_id_type=MESH)

    for i, row in enumerate(ITEMS):
        table[i] = pick(row)

    nt = (((1,), (1,)), ((), ()))
    blank = jnp.zeros((RANK, RANK * 8), F32)
    first = lax.dot_general(
        vectors[0], jnp.concatenate([inverse[0], blank], axis=0), nt,
        precision=lax.Precision.HIGHEST, preferred_element_type=F32,
    )
    second = lax.dot_general(
        vectors[1], jnp.concatenate([blank, inverse[1]], axis=0), nt,
        precision=lax.Precision.HIGHEST, preferred_element_type=F32,
    )
    blank = jnp.zeros((RANK, 2 * RANK), F32)
    part[...] = lax.dot_general(
        first, jnp.concatenate([first, blank], axis=0), nt,
        precision=lax.Precision.HIGHEST, preferred_element_type=F32,
    ) + lax.dot_general(
        second, jnp.concatenate([blank, second], axis=0), nt,
        precision=lax.Precision.HIGHEST, preferred_element_type=F32,
    )
    block_core[...] = jnp.zeros_like(block_core)

    pl.semaphore_wait(barrier, len(greeted))

    own_copies = []
    for i, (src, slot) in enumerate(own):
        copy = pltpu.make_async_remote_copy(
            src_ref=src, dst_ref=buf.at[slot], send_sem=own_send.at[i], recv_sem=recv_sem.at[slot],
            device_id=partner, device_id_type=MESH,
        )
        copy.start()
        own_copies.append(copy)

    def arrived(slot):
        pltpu.make_async_copy(buf.at[slot], buf.at[slot], recv_sem.at[slot]).wait()

    def panel_at(code):
        block = 2 * ((sy * (code % 4) + z + 4) % 4) + (code // 4 + flip) % 2
        return 4 * block + code // 8

    def send_of(i, word):
        way = word % 16
        src, dst = (word // 32) % 128, (word // 4096) % 128
        axis, turn = way // 2, 1 - 2 * (way % 2)
        dx = jnp.where(axis == 0, sx * turn, 0)
        dy = jnp.where(axis == 1, sy * turn, 0)
        dz = jnp.where(axis == 2, sy * turn, 0)
        dk = jnp.where(axis == 3, 1, 0)
        target = device((x + dx + 4) % 4, (y + dy + 4) % 4, (z + dz + 4) % 4, (k + dk) % 2)
        return src, pltpu.make_async_remote_copy(
            src_ref=buf.at[src], dst_ref=buf.at[dst], send_sem=send_sem.at[i],
            recv_sem=recv_sem.at[dst], device_id=target, device_id_type=MESH,
        )

    def pass_on(i, word):
        src, copy = send_of(i, word)

        @pl.when((word // 16) % 2 == 1)
        def _():
            arrived(src)

        @pl.when(word % 16 < 7)
        def _():
            copy.start()

    def moves(i, _):
        pass_on(i, table[i])
        return 0

    def sent(i, _):
        @pl.when(table[i] % 16 < 7)
        def _():
            pltpu.make_async_copy(buf.at[0], buf.at[0], send_sem.at[i]).wait()

        return 0

    def prepare(block):
        codes = pick(BLOCKS[block])
        for a in range(4):
            place = 4 * block + a
            arrived(OTHER + place)
            panel = panel_at((codes // (1 << (5 * a))) % 32)
            high, low = split(buf[jnp.where(diagonal == 1, place, COL_SLOT + place)])
            wide[pl.ds(a * RANK, RANK)] = high
            wide[pl.ds(256 + a * RANK, RANK)] = high
            wide[pl.ds(512 + a * RANK, RANK)] = low
            slot = slots[panel]
            pair = known[(slot // 2) % 2 * 8 + slot // 4]
            lane = lax.broadcasted_iota(I32, (RANK, 2 * RANK), 1) // RANK
            same = jnp.where(slot % 2 == a % 2, F32(1), F32(0))
            moved = pair * same + pltpu.roll(pair, RANK, axis=1) * (F32(1) - same)
            block_core[pl.ds(a * RANK, RANK), pl.ds((a // 2) * 128, 128)] = jnp.where(
                lane == a % 2, moved, F32(0)
            )
        high, low = split(block_core[...])
        scaled = jnp.dot(
            jnp.concatenate([high, low, high], axis=1), wide[...], preferred_element_type=F32
        )
        high, low = split(scaled)
        right[0:256] = high
        right[256:512] = high
        right[512:768] = low

    def tile_rows(j):
        h = k if j * TI < HALF else 1 - k
        return pl.ds(pl.multiple_of(h * HALF + (j * TI) % HALF, TI), TI)

    def tile(block, j):
        if j == 0:
            prepare(block)
        base = 4 * block + (0 if j * TI < HALF else OTHER)
        left = buf[base : base + 4, :, (j * TI) % HALF : (j * TI) % HALF + TI]
        high, low = split(left.reshape(256, TI))
        rows = tile_rows(j)
        acc[rows] = acc[rows] - lax.dot_general(
            jnp.concatenate([high, low, high], axis=0), right[...], (((0,), (0,)), ((), ())),
            preferred_element_type=F32,
        )

    mine = k * 8 + q
    row_copies = [
        pltpu.make_async_remote_copy(
            src_ref=part, dst_ref=by_row.at[6 - i], send_sem=row_send.at[i],
            recv_sem=row_recv.at[6 - i], device_id=peer, device_id_type=MESH,
        )
        for i, peer in enumerate(row_peers)
    ]
    keep = pltpu.make_async_copy(total, cores.at[mine], local_sem.at[5])
    col_copies = [
        pltpu.make_async_remote_copy(
            src_ref=total, dst_ref=cores.at[mine], send_sem=col_send.at[i],
            recv_sem=col_recv.at[i], device_id=peer, device_id_type=MESH,
        )
        for i, peer in enumerate(col_peers)
    ]
    half = cores.at[pl.ds(k * 8, 8)]
    exchange = pltpu.make_async_remote_copy(
        src_ref=half, dst_ref=half, send_sem=col_send.at[7], recv_sem=col_recv.at[7],
        device_id=partner, device_id_type=MESH,
    )
    settle = pltpu.make_async_copy(cores, known, local_sem.at[6])

    def give_share():
        for copy in row_copies:
            copy.start()

    def add_shares():
        for i in range(7):
            pltpu.make_async_copy(part, by_row.at[i], row_recv.at[i]).wait()
        summed = part[...]
        for i in range(7):
            summed = summed + by_row[i]
        total[...] = summed

    def give_total():
        keep.start()
        for copy in col_copies:
            copy.start()

    def give_half():
        keep.wait()
        for i in range(7):
            sender = k * 8 + (q + 7 - i) % 8
            pltpu.make_async_copy(total, cores.at[sender], col_recv.at[i]).wait()
        exchange.start()

    def take_half():
        exchange.wait_recv()
        settle.start()
        settle.wait()
        start_acc.wait()

    def opening(i, _):
        word = table[i]

        @pl.when(word % 16 < 8)
        def _():
            pass_on(i, word)

        for phase, action in enumerate((give_share, add_shares, give_total, give_half, take_half)):
            pl.when(word % 16 == 9 + phase)(action)
        return 0

    lax.fori_loop(0, SEGMENTS[0], opening, 0)
    tiles = ROWS // TI
    done = SEGMENTS[0]
    end = checked = 0
    for t, length in enumerate(SEGMENTS):
        end += length
        if end > done:
            lax.fori_loop(done, end, moves, 0)
            done = end
        if t in (4 * tiles, 7 * tiles):
            early = sum(SEGMENTS[: t - tiles])
            lax.fori_loop(checked, early, sent, 0)
            checked = early
        if t < 8 * tiles:
            tile(t // tiles, t % tiles)

    for copy in own_copies + row_copies + col_copies + [exchange]:
        copy.wait_send()

    lax.fori_loop(checked, NI, sent, 0)


def body(trailing, panel_factors, vectors_t, inverse_lower_factors, slot_of_panel):
    hbm = pl.BlockSpec(memory_space=pl.ANY)
    vmem = pl.BlockSpec(memory_space=pltpu.VMEM)
    dma = pltpu.SemaphoreType.DMA
    return pl.pallas_call(
        kernel,
        out_shape=pltpu.VMEM((ROWS, COLS), F32),
        in_specs=[hbm, hbm, vmem, vmem, pl.BlockSpec(memory_space=pltpu.SMEM)],
        out_specs=vmem,
        scratch_shapes=[
            pltpu.VMEM((SLOTS, RANK, HALF), F32),
            pltpu.VMEM((768, COLS), BF16),
            pltpu.VMEM((768, COLS), BF16),
            pltpu.VMEM((256, 256), F32),
            pltpu.VMEM((RANK, 2 * RANK), F32),
            pltpu.VMEM((7, RANK, 2 * RANK), F32),
            pltpu.VMEM((RANK, 2 * RANK), F32),
            pltpu.VMEM((16, RANK, 2 * RANK), F32),
            pltpu.VMEM((16, RANK, 2 * RANK), F32),
            pltpu.SMEM((NI,), I32),
            dma((7,)), dma((SLOTS,)), dma((NI,)), dma((4,)), dma((7,)), dma((7,)), dma((8,)), dma((8,)),
        ],
        compiler_params=pltpu.CompilerParams(
            collective_id=0, has_side_effects=True, vmem_limit_bytes=55 * 2**20
        ),
        name="update",
    )(trailing, panel_factors, vectors_t, inverse_lower_factors, slot_of_panel)


def solution(mesh):
    return jax.shard_map(
        body,
        mesh=mesh,
        in_specs=(
            P("row", "col"),
            P("col", "row"),
            P("col", None, None),
            P("col", "row", None),
            P(),
        ),
        out_specs=P("row", "col"),
        check_vma=False,
    )
```
